32 devices in a mesh: dp: 4 (over z), tensor: 8 (over y, x, core).
Axes of the slice: x: 2, y: 2, z: 4, core: 2. Of those that a mesh axis runs over, the one named last changes fastest.
Arguments:
- activations: bfloat16 [3072, 4096], P('dp', 'tensor'), may hold values from -6 to 6
- out_grads_t: bfloat16 [5504, 3072], P('tensor', 'dp'), may hold values from -6 to 6
- in_basis: bfloat16 [4096, 4096], P(None, 'tensor'), may hold values from -0.09375 to 0.09375
- out_basis_t: bfloat16 [5504, 5504], P('tensor'), may hold values from -0.078125 to 0.078125
- query_proj: bfloat16 [4, 5504, 4096], P(None, 'tensor', 'dp'), may hold values from -6 to 6
- eigvals: float32 [5504, 4096], P('tensor', 'dp'), may hold values from 0.05 to 5
- damping: float32 [1], replicated, may hold values from 0.05 to 0.2
- lengths: int32 [24], P('dp'), may hold values from 1 to 128, 1920 in all
Outputs:
- scores: float32 [24, 4], P('dp')
The draws below stay inside these ranges and needn't reach their ends.
Inputs may be any that keep to these rules, and one draw needn't show every extreme that they name: `lengths`: the largest token count is exactly 128.
All inputs are finite; a program needn't handle non-finite values. No bound on the sum of `lengths` on one device may be relied on, other than what follows from the above.
Results may differ from the reference program's by a relative error of at most 0.006.
Values may be sent and summed in bfloat16 or wider, within the bound.
A program may use at most 128 MiB of HBM per device.

```python
import math
import jax
import jax.numpy as jnp
import numpy as np
from jax import lax

D = 4096
FF = 5504
QUERIES = 4
SEQ_LEN = 128
SEQS = 24
TOKENS = 3072


def steps_of(rng, shape, shards, least, top_value):
    def one(dim, parts):
        heights = jax.random.uniform(jax.random.fold_in(jax.random.fold_in(rng, 6), dim), (parts,), jnp.float32, least / len(shards), top_value / len(shards))
        return jnp.repeat(jnp.exp(heights), shape[dim] // parts).reshape((-1,) + (1,) * (len(shape) - dim - 1))

    factor_of = one(*shards[0])
    for cut in shards[1:]:
        factor_of = factor_of * one(*cut)
    return factor_of


def split_up(count, total, limit, lean):
    loads = [(1 << 20) // math.isqrt(standing ** lean) + 1 for standing in range(2, count + 1)]
    spare, counts = total - limit - (count - 1), [1] * (count - 1)
    while spare > 0:
        candidates = [i for i in range(count - 1) if counts[i] < limit]
        mass, budget = sum([loads[i] for i in candidates]), spare
        for i in candidates:
            more = min(limit - counts[i], max(1, budget * loads[i] // mass), spare)
            counts[i] = counts[i] + more
            spare = spare - more
    return np.array([limit] + counts)


def ragged_sizes(rng, count, total, limit, slope):
    if count == 2:
        one = jax.random.randint(rng, (), max(1, total - limit), min(limit, total - 1) + 1)
        return jnp.stack([one, total - one])
    sizes = jnp.asarray(split_up(count, total, limit, slope), jnp.int32)
    twos = (count - 1) // 2
    donor, taker = sizes[1:1 + 2 * twos:2], sizes[2:2 + 2 * twos:2]
    slack = jnp.minimum(donor - 1, limit - taker)
    passed = jax.random.randint(jax.random.fold_in(rng, 1), (twos,), 0, 1 << 20) % (slack + 1)
    sizes = sizes.at[1:1 + 2 * twos:2].set(donor - passed).at[2:2 + 2 * twos:2].set(taker + passed)
    return sizes[jax.random.permutation(jax.random.fold_in(rng, 2), count)]


def gaussian(own_key, dims, deviation, bound, shards=(), kind=jnp.bfloat16):
    values = deviation * jax.random.normal(own_key, dims, jnp.float32)
    if shards:
        values = values * steps_of(own_key, dims, shards, -0.22, 0.18)
    return jnp.clip(values, -bound, bound).astype(kind)


def setup_inputs(seed: int = 0) -> dict:
    streams_of = jax.random.split(jax.random.key(seed), 9)
    return {
        "activations": gaussian(streams_of[0], (TOKENS, D), 1.0, 6.0, ((0, 4), (1, 8))),
        "out_grads_t": gaussian(streams_of[1], (FF, TOKENS), 1.0, 6.0, ((0, 8), (1, 4))),
        "in_basis": gaussian(streams_of[2], (D, D), D ** -0.5, 0.09375, ((1, 8),)),
        "out_basis_t": gaussian(streams_of[3], (FF, FF), FF ** -0.5, 0.078125, ((0, 8),)),
        "query_proj": gaussian(streams_of[4], (QUERIES, FF, D), 1.0, 6.0, ((1, 8), (2, 4))),
        "eigvals": jnp.clip(jnp.exp(math.log(5.0) - 4.6051702 * jax.random.uniform(streams_of[5], (FF, D), jnp.float32) ** steps_of(streams_of[5], (FF, D), ((0, 8), (1, 4)), -0.2, 0.2)), 0.05, 5.0),
        "damping": jnp.clip(jax.random.uniform(streams_of[6], (1,), jnp.float32, 0.05, 0.2), 0.05, 0.2),
        "lengths": ragged_sizes(streams_of[7], SEQS, SEQS * SEQ_LEN * 5 // 8, SEQ_LEN, 1).astype(jnp.int32),
    }


def reference(activations, out_grads_t, in_basis, out_basis_t, query_proj, eigvals, damping, lengths):
    act_proj = jnp.dot(activations, in_basis, preferred_element_type=jnp.float32).astype(jnp.bfloat16)
    grad_full = jnp.dot(out_basis_t, out_grads_t, preferred_element_type=jnp.float32)
    position = lax.broadcasted_iota(jnp.int32, (SEQS, SEQ_LEN), 1)
    keep = (position < lengths[:, None]).astype(jnp.float32).reshape(1, SEQS * SEQ_LEN)
    grad_proj = (grad_full * keep).astype(jnp.bfloat16)
    scaled = (query_proj.astype(jnp.float32) / (eigvals + damping[0])).astype(jnp.bfloat16)
    scaled_wide = scaled.astype(jnp.float32)

    def one_sequence(index):
        start = (index * SEQ_LEN).astype(jnp.int32)
        grad_cols = lax.dynamic_slice_in_dim(grad_proj, start, SEQ_LEN, 1)
        act_rows = lax.dynamic_slice_in_dim(act_proj, start, SEQ_LEN, 0)
        projected = jnp.dot(grad_cols, act_rows, preferred_element_type=jnp.float32)
        return jnp.einsum("ij,qij->q", projected, scaled_wide)

    totals = lax.map(one_sequence, jnp.arange(SEQS, dtype=jnp.int32))
    return totals * ((D * FF * SEQ_LEN) ** -0.5)
```

```python
import functools

import jax
import jax.numpy as jnp
from jax import lax
from jax.experimental import pallas as pl
from jax.experimental.pallas import tpu as pltpu
from jax.sharding import PartitionSpec as P


def generic(activations, out_grads_t, in_basis, out_basis_t, query_proj, eigvals, damping, lengths):
    bf16, f32 = jnp.bfloat16, jnp.float32
    seq_count = lengths.shape[0]
    full_act = lax.all_gather(activations, "tensor", axis=1, tiled=True)
    token_rows = full_act.shape[0]
    seq_len = token_rows // seq_count
    act_local = jnp.dot(full_act, in_basis, preferred_element_type=f32).astype(bf16)
    act_full = lax.all_gather(act_local, "tensor", axis=1, tiled=True)
    features = act_full.shape[1]
    act_proj = lax.all_to_all(act_full, "dp", split_axis=1, concat_axis=0, tiled=True)
    grad_full = jnp.dot(
        out_basis_t, lax.all_gather(out_grads_t, "tensor", axis=0, tiled=True), preferred_element_type=f32
    )
    position = lax.broadcasted_iota(jnp.int32, (seq_count, seq_len), 1)
    keep = (position < lengths[:, None]).astype(f32).reshape(1, token_rows)
    grad_local = (grad_full * keep).astype(bf16)
    grad_proj = lax.all_gather(grad_local, "dp", axis=1, tiled=True)
    scaled = (query_proj.astype(f32) / (eigvals + damping[0])).astype(bf16)
    mixed = jnp.einsum("td,qjd->qjt", act_proj, scaled, preferred_element_type=f32)
    weighted = mixed * grad_proj.astype(f32)[None, :, :]
    query_count, width, tokens = weighted.shape
    partial_value = jnp.sum(weighted.reshape(query_count, width, tokens // seq_len, seq_len), axis=(1, 3)).T
    totals = lax.psum(partial_value, ("dp", "tensor"))
    mine = lax.dynamic_slice_in_dim(totals, lax.axis_index("dp") * seq_count, seq_count, 0)
    norm_factor = (features * out_basis_t.shape[1] * seq_len) ** (-0.5)
    return mine * norm_factor


MESH = pl.DeviceIdType.MESH


def kernel(
    act_ref, og_ref, in_ref, out_ref, query_ref, eig_ref, len_ref, damp_ref, res_ref,
    og_all, act_all, in_b, out_b, scaled, eig, a_all, a_part, a_loc, a_acc, g_all, g_acc, csum, tiles, got_z, got_p,
    load_sem, gs_send, gs_recv, up_send, up_recv, dn_send, dn_recv, xp_send, xp_recv, xz_send, xz_recv,
    rz_send, rz_recv, rp_send, rp_recv,
):
    bf16, f32 = jnp.bfloat16, jnp.float32
    z, j = lax.axis_index("dp"), lax.axis_index("tensor")
    members, rows, feats = act_all.shape
    planes, units, width, unit = g_all.shape
    depth = out_b.shape[1]
    queries, span = scaled.shape[0], scaled.shape[2]
    cols = a_loc.shape[2]
    part = unit // members
    pairs = units // 2
    group = span // cols
    half_planes = planes // 2
    pieces = [(0, 1), (1, 1)] + [(2 * n, 2) for n in range(1, pairs)]
    jx = j + 2 - 4 * lax.rem(j // 2, 2)
    jy = j + 4 - 8 * (j // 4)
    jd = jx + 4 - 8 * (j // 4)

    def mate(k):
        return k + 1 - 2 * lax.rem(k, 2)

    jp = mate(j)

    loads = [
        pltpu.make_async_copy(og_ref, og_all.at[pl.ds(pl.multiple_of(j * width, 16), width), :], load_sem.at[0]),
        pltpu.make_async_copy(act_ref, act_all.at[j], load_sem.at[1]),
        pltpu.make_async_copy(query_ref, scaled, load_sem.at[2]),
        pltpu.make_async_copy(eig_ref, eig, load_sem.at[3]),
        pltpu.make_async_copy(out_ref, out_b, load_sem.at[4]),
        pltpu.make_async_copy(in_ref, in_b, load_sem.at[5]),
    ]
    for load in loads:
        load.start()

    barrier = pltpu.get_barrier_semaphore()
    for step in range(1, members):
        pl.semaphore_signal(barrier, inc=1, device_id={"tensor": lax.rem(j + step, members)}, device_id_type=MESH)
    for step in range(1, planes):
        pl.semaphore_signal(barrier, inc=1, device_id={"dp": lax.rem(z + step, planes)}, device_id_type=MESH)

    def meet():
        pl.semaphore_wait(barrier, members + planes - 2)

    class Gather:
        def __init__(self, op, view, own):
            self.op, self.view, self.own = op, view, own
            self.plan = [
                (j, 0, jx), (j, 1, jx), (jy, 1, jx),
                (j, 1, jy), (j, 0, jy), (jx, 0, jy),
                (j, None, jp), (jx, None, jp), (jy, None, jp), (jd, 0, jp), (jd, 1, jp),
            ]
            self.landed = [
                (jx, 0), (jx, 1), (jd, 1),
                (jy, 1), (jy, 0), (jd, 0),
                (jp, None), (mate(jx), None), (mate(jy), None), (mate(jd), 0), (mate(jd), 1),
            ]

        def copy(self, slot):
            block, half, target = self.plan[slot]
            src = self.own(half) if slot in (0, 1, 3, 4, 6) else self.view(block, half)
            return pltpu.make_async_remote_copy(
                src_ref=src, dst_ref=self.view(block, half), send_sem=gs_send.at[self.op, slot],
                recv_sem=gs_recv.at[self.op, slot], device_id={"tensor": target}, device_id_type=MESH,
            )

        def start(self, *slots):
            for slot in slots:
                self.copy(slot).start()

        def arrive(self, *slots):
            for slot in slots:
                block, half = self.landed[slot]
                view = self.view(block, half)
                pltpu.make_async_remote_copy(
                    src_ref=view, dst_ref=view, send_sem=gs_send.at[self.op, slot],
                    recv_sem=gs_recv.at[self.op, slot], device_id={"tensor": jp}, device_id_type=MESH,
                ).wait_recv()

        def begin(self):
            self.start(0, 3, 1, 4, 6)

        def relay(self):
            self.arrive(0)
            self.start(5)
            self.arrive(3)
            self.start(2)

        def near(self):
            self.arrive(1)
            self.start(7)
            self.arrive(4)
            self.start(8)

        def far(self):
            self.arrive(5)
            self.start(9)
            self.arrive(2)
            self.start(10)

        def finish(self):
            self.arrive(6, 7, 8, 9, 10)

        def drain(self):
            for slot in range(len(self.plan)):
                self.copy(slot).wait_send()

    cut = (width // 2 + 15) // 16 * 16

    def og_rows(h):
        return (0, width) if h is None else ((0, cut), (cut, width - cut))[h]

    def og_gather(op, first, count):
        lanes = pl.ds(first * unit, count * unit)

        def view(k, h):
            top, size = og_rows(h)
            return og_all.at[pl.ds(pl.multiple_of(k * width + top, 16), size), lanes]

        return Gather(op, view, lambda h: og_ref.at[pl.ds(*og_rows(h)), lanes])

    def act_gather(op, r):
        def at(h):
            size = 2 * unit if h is None else unit
            return pl.ds(2 * unit * r + unit * (h or 0), size)

        return Gather(op, lambda k, h: act_all.at[k, at(h), :], lambda h: act_ref.at[at(h), :])

    def acts_gather(op, u):
        def view(k, h):
            at = pl.ds(pl.multiple_of(k * part, 16), part)
            if h is None:
                return a_all.at[u, :, at, :]
            return a_all.at[u, pl.ds(h * half_planes, half_planes), at, :]

        return Gather(op, view, lambda h: view(j, h))

    og = [og_gather(n, *piece) for n, piece in enumerate(pieces)]
    act = [act_gather(len(og) + r, r) for r in range(pairs)]
    acts = [acts_gather(len(og) + len(act) + u, u) for u in range(units)]

    def scale_all():
        csum[...] = jnp.zeros_like(csum)
        loads[2].wait()
        loads[3].wait()
        step_rows = 16

        def scale(i, carry):
            at = pl.ds(pl.multiple_of(i * step_rows, step_rows), step_rows)
            below = eig[at, :] + damp_ref[0]
            for q in range(queries):
                scaled[q, at, :] = (scaled[q, at, :].astype(f32) / below).astype(bf16)
            return carry

        lax.fori_loop(0, width // step_rows, scale, 0)

    def chain(n, block, sends, recvs, to):
        first, count = pieces[n]
        view = g_all.at[block, pl.ds(first, count)]
        return pltpu.make_async_remote_copy(
            src_ref=view, dst_ref=view, send_sem=sends.at[block, n], recv_sem=recvs.at[block, n],
            device_id={"dp": to}, device_id_type=MESH,
        )

    def up(block, n):
        return chain(n, block, up_send, up_recv, lax.rem(z + 1, planes))

    def down(block, n):
        return chain(n, block, dn_send, dn_recv, lax.rem(z + planes - 1, planes))

    def service(level, n):
        @pl.when(z - level >= 0)
        def _():
            up(z - level, n).wait_recv()

        @pl.when((z - level >= 0) & (z < planes - 1))
        def _():
            up(z - level, n).start()

        @pl.when(z + level < planes)
        def _():
            down(z + level, n).wait_recv()

        @pl.when((z + level < planes) & (z > 0))
        def _():
            down(z + level, n).start()

    k_tile = 6 * unit
    k_full = depth // k_tile

    def project(n):
        first, count = pieces[n]
        wide = count * unit
        at, to = pl.ds(first * unit, wide), pl.ds(0, wide)
        k_rest = depth - k_full * k_tile
        if k_rest:
            g_acc[:, to] = jnp.dot(
                out_b[:, pl.ds(k_full * k_tile, k_rest)], og_all[pl.ds(k_full * k_tile, k_rest), at],
                preferred_element_type=f32,
            )
        else:
            g_acc[:, to] = jnp.zeros((width, wide), f32)

        def inner(k, c):
            deep = pl.ds(pl.multiple_of(k * k_tile, k_tile), k_tile)
            g_acc[:, to] += jnp.dot(out_b[:, deep], og_all[deep, at], preferred_element_type=f32)
            return c

        lax.fori_loop(0, k_full, inner, 0)
        lane = lax.broadcasted_iota(jnp.int32, (1, unit), 1)
        for i in range(count):
            keep = (lane < len_ref[first + i]).astype(f32)
            g_all[z, first + i] = (g_acc[:, pl.ds(i * unit, unit)] * keep).astype(bf16)

        @pl.when(z < planes - 1)
        def _():
            up(z, n).start()

        @pl.when(z > 0)
        def _():
            down(z, n).start()

    def contract(r):
        at = pl.ds(2 * unit * r, 2 * unit)
        a_acc[...] = jnp.zeros_like(a_acc)

        def body(k, carry):
            deep = pl.ds(pl.multiple_of(k * feats, feats), feats)
            a_acc[...] += jnp.dot(act_all[k, at, :], in_b[deep, :], preferred_element_type=f32)
            return carry

        lax.fori_loop(0, members, body, 0)
        for s in range(2):
            a_loc[2 * r + s] = a_acc[pl.ds(s * unit, unit), :].astype(bf16)

    def own_rows(k):
        return pl.ds(pl.multiple_of(k * part, 16), part)

    def spread_to(r, to):
        return pltpu.make_async_remote_copy(
            src_ref=a_loc.at[pl.ds(2 * r, 2), own_rows(to), :],
            dst_ref=a_part.at[r, j], send_sem=xp_send.at[r, to], recv_sem=xp_recv.at[r, j],
            device_id={"tensor": to}, device_id_type=MESH,
        )

    def spread_from(r, k):
        return pltpu.make_async_remote_copy(
            src_ref=a_part.at[r, k], dst_ref=a_part.at[r, k], send_sem=xp_send.at[r, k], recv_sem=xp_recv.at[r, k],
            device_id={"tensor": k}, device_id_type=MESH,
        )

    def spread(r):
        for step in range(1, members):
            spread_to(r, lax.rem(j + step, members)).start()
        a_part[r, j] = a_loc[pl.ds(2 * r, 2), own_rows(j), :]

    def lift_to(r, to, g):
        lane = pl.ds(g * cols, cols)
        return pltpu.make_async_remote_copy(
            src_ref=a_part.at[r, to * group + g], dst_ref=a_all.at[pl.ds(2 * r, 2), z, own_rows(j), lane],
            send_sem=xz_send.at[r, to, g], recv_sem=xz_recv.at[r, z, g], device_id={"dp": to}, device_id_type=MESH,
        )

    def lift_from(r, k, g):
        lane = pl.ds(g * cols, cols)
        view = a_all.at[pl.ds(2 * r, 2), k, own_rows(j), lane]
        return pltpu.make_async_remote_copy(
            src_ref=view, dst_ref=view, send_sem=xz_send.at[r, k, g], recv_sem=xz_recv.at[r, k, g],
            device_id={"dp": k}, device_id_type=MESH,
        )

    def lift(r):
        for step in range(1, members):
            spread_from(r, lax.rem(j + step, members)).wait_recv()
        for step in range(1, planes):
            for g in range(group):
                lift_to(r, lax.rem(z + step, planes), g).start()
        for g in range(group):
            a_all[pl.ds(2 * r, 2), z, own_rows(j), pl.ds(g * cols, cols)] = a_part[r, z * group + g]

    def lifted(r):
        for step in range(1, planes):
            for g in range(group):
                lift_from(r, lax.rem(z + step, planes), g).wait_recv()

    def score(u):
        def body(h, carry):
            block = a_all[u, pl.ds(2 * h, 2)].reshape(2 * unit, span)
            for q in range(queries):
                mixed = lax.dot_general(
                    scaled[q], block, (((1,), (1,)), ((), ())), preferred_element_type=f32
                )
                for b in range(2):
                    csum[2 * h + b, u, pl.ds(q, 1), :] = jnp.sum(
                        mixed[:, b * unit:(b + 1) * unit] * g_all[2 * h + b, u].astype(f32), axis=0, keepdims=True
                    )
            return carry

        lax.fori_loop(0, half_planes, body, 0)

    def loaded(*which):
        for n in which:
            loads[n].wait()

    meet()
    og[0].begin()
    scale_all()
    og[0].relay()
    og[1].begin()
    og[0].near()
    og[0].far()
    og[0].finish()
    loaded(0, 4)
    project(0)
    og[1].relay()
    og[2].begin()
    og[1].near()
    og[1].far()
    og[1].finish()
    project(1)
    og[2].relay()
    act[0].begin()
    og[2].near()
    service(1, 0)
    og[2].far()
    og[2].finish()
    project(2)
    service(2, 0)
    act[0].relay()
    act[1].begin()
    act[0].near()
    service(1, 1)
    act[0].far()
    act[0].finish()
    loaded(1, 5)
    contract(0)
    spread(0)
    act[1].relay()
    og[3].begin()
    service(3, 0)
    act[1].near()
    service(2, 1)
    act[1].far()
    act[1].finish()
    contract(1)
    spread(1)
    lift(0)
    og[3].relay()
    act[2].begin()
    service(1, 2)
    og[3].near()
    service(3, 1)
    og[3].far()
    og[3].finish()
    project(3)
    lift(1)
    act[2].relay()
    lifted(0)
    acts[0].begin()
    act[2].near()
    service(2, 2)
    act[2].far()
    act[2].finish()
    contract(2)
    spread(2)
    acts[0].relay()
    acts[1].begin()
    acts[0].near()
    acts[0].far()
    acts[0].finish()
    lift(2)
    service(3, 2)
    score(0)
    service(1, 3)
    acts[1].relay()
    lifted(1)
    acts[2].begin()
    acts[1].near()
    acts[1].far()
    acts[1].finish()
    service(2, 3)
    score(1)
    acts[2].relay()
    acts[3].begin()
    acts[2].near()
    acts[2].far()
    acts[2].finish()
    score(2)
    acts[3].relay()
    lifted(2)
    acts[4].begin()
    acts[3].near()
    acts[3].far()
    acts[3].finish()
    score(3)
    acts[4].relay()
    acts[5].begin()
    acts[4].near()
    acts[4].far()
    acts[4].finish()
    service(3, 3)
    score(4)
    acts[5].relay()
    acts[5].near()
    acts[5].far()
    acts[5].finish()
    score(5)
    per = res_ref.shape[1]
    lane_at = lax.broadcasted_iota(jnp.int32, (8, per), 1)
    for b in range(planes):
        tile = jnp.zeros((8, per), f32)
        for u in range(units):
            total = jnp.sum(csum[b, u], axis=1, keepdims=True)
            tile = tile + jnp.where(lane_at == u, total, 0.0)
        tiles[b] = tile

    def fold(to):
        return pltpu.make_async_remote_copy(
            src_ref=tiles.at[to], dst_ref=got_z.at[z], send_sem=rz_send.at[to], recv_sem=rz_recv.at[z],
            device_id={"dp": to}, device_id_type=MESH,
        )

    def fold_from(k):
        return pltpu.make_async_remote_copy(
            src_ref=got_z.at[k], dst_ref=got_z.at[k], send_sem=rz_send.at[k], recv_sem=rz_recv.at[k],
            device_id={"dp": k}, device_id_type=MESH,
        )

    def fold_all():
        for step in range(1, planes):
            fold(lax.rem(z + step, planes)).start()
        got_z[z] = tiles[z]
        for step in range(1, planes):
            fold_from(lax.rem(z + step, planes)).wait_recv()
        total = got_z[0]
        for b in range(1, planes):
            total = total + got_z[b]
        got_p[j] = total

    def share(to):
        return pltpu.make_async_remote_copy(
            src_ref=got_p.at[j], dst_ref=got_p.at[j], send_sem=rp_send.at[to], recv_sem=rp_recv.at[j],
            device_id={"tensor": to}, device_id_type=MESH,
        )

    def share_from(k):
        return pltpu.make_async_remote_copy(
            src_ref=got_p.at[k], dst_ref=got_p.at[k], send_sem=rp_send.at[k], recv_sem=rp_recv.at[k],
            device_id={"tensor": k}, device_id_type=MESH,
        )

    def share_all():
        for step in range(1, members):
            share(lax.rem(j + step, members)).start()
        for step in range(1, members):
            share_from(lax.rem(j + step, members)).wait_recv()
        total = got_p[0]
        for k in range(1, members):
            total = total + got_p[k]
        res_ref[...] = total

    def drain_all():
        for op in og + act + acts:
            op.drain()
        for level in range(planes):
            for n in range(len(pieces)):
                @pl.when((z - level >= 0) & (z < planes - 1))
                def _():
                    up(z - level, n).wait_send()

                @pl.when((z + level < planes) & (z > 0))
                def _():
                    down(z + level, n).wait_send()
        for step in range(1, members):
            to = lax.rem(j + step, members)
            for r in range(pairs):
                spread_to(r, to).wait_send()
            share(to).wait_send()
        for step in range(1, planes):
            to = lax.rem(z + step, planes)
            for r in range(pairs):
                for g in range(group):
                    lift_to(r, to, g).wait_send()
            fold(to).wait_send()

    fold_all()
    share_all()
    drain_all()


def fits(planes, members, activations, out_grads_t, in_basis, query_proj, seq_count):
    rows, feats = activations.shape
    width, tokens = out_grads_t.shape
    cols, span = in_basis.shape[1], query_proj.shape[2]
    unit = rows // seq_count
    return (
        members == 8 and planes == 4 and rows == tokens and rows == unit * seq_count and unit == 16 * members
        and seq_count == 6 and feats % 128 == 0 and cols % 128 == 0 and span % cols == 0 and span == 2 * cols
        and width % 16 == 0 and width > 32 and query_proj.shape[0] <= 8
    )


def local(planes, members, activations, out_grads_t, in_basis, out_basis_t, query_proj, eigvals, damping, lengths):
    seq_count = lengths.shape[0]
    if not fits(planes, members, activations, out_grads_t, in_basis, query_proj, seq_count):
        return generic(activations, out_grads_t, in_basis, out_basis_t, query_proj, eigvals, damping, lengths)
    bf16, f32 = jnp.bfloat16, jnp.float32
    rows, feats = activations.shape
    width, tokens = out_grads_t.shape
    features, cols = in_basis.shape
    depth = out_basis_t.shape[1]
    queries, _, span = query_proj.shape
    unit = rows // seq_count
    part, pairs, group = unit // members, seq_count // 2, span // cols
    pieces = pairs + 1
    ops = pieces + pairs + seq_count
    any_space = pl.BlockSpec(memory_space=pl.ANY)
    vmem = pl.BlockSpec(memory_space=pltpu.VMEM)
    smem = pl.BlockSpec(memory_space=pltpu.SMEM)
    dma = pltpu.SemaphoreType.DMA
    res = pl.pallas_call(
        kernel,
        out_shape=jax.ShapeDtypeStruct((8, 128), f32),
        in_specs=[any_space] * 6 + [smem, smem],
        out_specs=vmem,
        scratch_shapes=[
            pltpu.VMEM((members * width, tokens), bf16),
            pltpu.VMEM((members, rows, feats), bf16),
            pltpu.VMEM((features, cols), bf16),
            pltpu.VMEM((width, depth), bf16),
            pltpu.VMEM((queries, width, span), bf16),
            pltpu.VMEM((width, span), f32),
            pltpu.VMEM((seq_count, planes, unit, span), bf16),
            pltpu.VMEM((pairs, members, 2, part, cols), bf16),
            pltpu.VMEM((seq_count, unit, cols), bf16),
            pltpu.VMEM((2 * unit, cols), f32),
            pltpu.VMEM((planes, seq_count, width, unit), bf16),
            pltpu.VMEM((width, 2 * unit), f32),
            pltpu.VMEM((planes, seq_count, 8, unit), f32),
            pltpu.VMEM((planes, 8, 128), f32),
            pltpu.VMEM((planes, 8, 128), f32),
            pltpu.VMEM((members, 8, 128), f32),
            dma((6,)), dma((ops, 11)), dma((ops, 11)),
            dma((planes, pieces)), dma((planes, pieces)), dma((planes, pieces)), dma((planes, pieces)),
            dma((pairs, members)), dma((pairs, members)), dma((pairs, planes, group)), dma((pairs, planes, group)),
            dma((planes,)), dma((planes,)), dma((members,)), dma((members,)),
        ],
        compiler_params=pltpu.CompilerParams(
            collective_id=0, has_side_effects=True, vmem_limit_bytes=63 * 1024 * 1024
        ),
    )(activations, out_grads_t, in_basis, out_basis_t, query_proj, eigvals, lengths, damping)
    norm_factor = (features * depth * unit) ** (-0.5)
    return res[:queries, :seq_count].T * norm_factor


def solution(mesh):
    placed = (
        P("dp", "tensor"),
        P("tensor", "dp"),
        P(None, "tensor"),
        P("tensor", None),
        P(None, "tensor", "dp"),
        P("tensor", "dp"),
        P(),
        P("dp"),
    )
    return jax.shard_map(
        functools.partial(local, mesh.shape["dp"], mesh.shape["tensor"]), mesh=mesh, in_specs=placed, out_specs=P("dp", None), check_vma=False
    )
```

```python
import functools

import jax
import jax.numpy as jnp
from jax import lax
from jax.experimental import pallas as pl
from jax.experimental.pallas import tpu as pltpu
from jax.sharding import PartitionSpec as P


def generic(activations, out_grads_t, in_basis, out_basis_t, query_proj, eigvals, damping, lengths):
    bf16, f32 = jnp.bfloat16, jnp.float32
    seq_count = lengths.shape[0]
    full_act = lax.all_gather(activations, "tensor", axis=1, tiled=True)
    token_rows = full_act.shape[0]
    seq_len = token_rows // seq_count
    act_local = jnp.dot(full_act, in_basis, preferred_element_type=f32).astype(bf16)
    act_full = lax.all_gather(act_local, "tensor", axis=1, tiled=True)
    features = act_full.shape[1]
    act_proj = lax.all_to_all(act_full, "dp", split_axis=1, concat_axis=0, tiled=True)
    grad_full = jnp.dot(
        out_basis_t, lax.all_gather(out_grads_t, "tensor", axis=0, tiled=True), preferred_element_type=f32
    )
    position = lax.broadcasted_iota(jnp.int32, (seq_count, seq_len), 1)
    keep = (position < lengths[:, None]).astype(f32).reshape(1, token_rows)
    grad_local = (grad_full * keep).astype(bf16)
    grad_proj = lax.all_gather(grad_local, "dp", axis=1, tiled=True)
    scaled = (query_proj.astype(f32) / (eigvals + damping[0])).astype(bf16)
    mixed = jnp.einsum("td,qjd->qjt", act_proj, scaled, preferred_element_type=f32)
    weighted = mixed * grad_proj.astype(f32)[None, :, :]
    query_count, width, tokens = weighted.shape
    partial_value = jnp.sum(weighted.reshape(query_count, width, tokens // seq_len, seq_len), axis=(1, 3)).T
    totals = lax.psum(partial_value, ("dp", "tensor"))
    mine = lax.dynamic_slice_in_dim(totals, lax.axis_index("dp") * seq_count, seq_count, 0)
    norm_factor = (features * out_basis_t.shape[1] * seq_len) ** (-0.5)
    return mine * norm_factor


MESH = pl.DeviceIdType.MESH


def kernel(
    act_ref, og_ref, in_ref, out_ref, query_ref, eig_ref, len_ref, damp_ref, res_ref,
    og_all, act_all, in_b, out_b, scaled, eig, a_all, a_part, a_loc, a_acc, g_all, g_acc, csum, tiles, got_z, got_p,
    load_sem, gs_send, gs_recv, up_send, up_recv, dn_send, dn_recv, xp_send, xp_recv, xz_send, xz_recv,
    rz_send, rz_recv, rp_send, rp_recv,
):
    bf16, f32 = jnp.bfloat16, jnp.float32
    z, j = lax.axis_index("dp"), lax.axis_index("tensor")
    members, rows, feats = act_all.shape
    planes, units, width, unit = g_all.shape
    depth = out_b.shape[1]
    queries, span = scaled.shape[0], scaled.shape[2]
    cols = a_loc.shape[2]
    part = unit // members
    pairs = units // 2
    group = span // cols
    half_planes = planes // 2
    pieces = [(0, 1), (1, 1)] + [(2 * n, 2) for n in range(1, pairs)]
    jx = j + 2 - 4 * lax.rem(j // 2, 2)
    jy = j + 4 - 8 * (j // 4)
    jd = jx + 4 - 8 * (j // 4)

    def mate(k):
        return k + 1 - 2 * lax.rem(k, 2)

    jp = mate(j)

    loads = [
        pltpu.make_async_copy(og_ref, og_all.at[pl.ds(pl.multiple_of(j * width, 16), width), :], load_sem.at[0]),
        pltpu.make_async_copy(act_ref, act_all.at[j], load_sem.at[1]),
        pltpu.make_async_copy(query_ref, scaled, load_sem.at[2]),
        pltpu.make_async_copy(eig_ref, eig, load_sem.at[3]),
        pltpu.make_async_copy(out_ref, out_b, load_sem.at[4]),
        pltpu.make_async_copy(in_ref, in_b, load_sem.at[5]),
    ]
    for load in loads:
        load.start()

    barrier = pltpu.get_barrier_semaphore()
    for step in range(1, members):
        pl.semaphore_signal(barrier, inc=1, device_id={"tensor": lax.rem(j + step, members)}, device_id_type=MESH)
    for step in range(1, planes):
        pl.semaphore_signal(barrier, inc=1, device_id={"dp": lax.rem(z + step, planes)}, device_id_type=MESH)

    def meet():
        pl.semaphore_wait(barrier, members + planes - 2)

    class Gather:
        def __init__(self, op, view, own, several):
            self.op, self.view, self.own, self.several = op, view, own, several
            self.plan = [
                (j, 0, jx), (j, 1, jx), (jy, 1, jx),
                (j, 1, jy), (j, 0, jy), (jx, 0, jy),
                (j, None, jp), (jx, None, jp), (jy, None, jp), (jd, 0, jp), (jd, 1, jp),
            ]
            self.lane = (0, 2, 3, 1, 2, 3, 4, 4, 4, 5, 5)

        def copy(self, slot):
            block, half, target = self.plan[slot]
            src = self.own(half) if slot in (0, 1, 3, 4, 6) else self.view(block, half)
            return pltpu.make_async_remote_copy(
                src_ref=src, dst_ref=self.view(block, half), send_sem=gs_send.at[self.op],
                recv_sem=gs_recv.at[self.op, self.lane[slot]], device_id={"tensor": target}, device_id_type=MESH,
            )

        def start(self, *slots):
            for slot in slots:
                self.copy(slot).start()

        def arrive(self, lane, view):
            pltpu.make_async_remote_copy(
                src_ref=view, dst_ref=view, send_sem=gs_send.at[self.op],
                recv_sem=gs_recv.at[self.op, lane], device_id={"tensor": jp}, device_id_type=MESH,
            ).wait_recv()

        def begin(self):
            self.start(0, 3, 1, 4, 6)

        def open(self):
            self.start(0, 3)

        def extend(self):
            self.start(1, 4, 6)

        def relay(self):
            self.arrive(0, self.view(jx, 0))
            self.start(5)
            self.arrive(1, self.view(jy, 1))
            self.start(2)

        def near(self):
            self.arrive(2, self.view(jx, None))
            self.start(7, 8)

        def far(self):
            self.arrive(3, self.view(jd, None))
            self.start(9, 10)

        def paired(self):
            self.arrive(4, self.several(3))

        def finish(self):
            self.arrive(5, self.view(mate(jd), None))

        def drain(self):
            view = self.several(len(self.plan) - 4)
            pltpu.make_async_remote_copy(
                src_ref=view, dst_ref=view, send_sem=gs_send.at[self.op],
                recv_sem=gs_recv.at[self.op, 0], device_id={"tensor": jp}, device_id_type=MESH,
            ).wait_send()

    cut = (width // 2 + 15) // 16 * 16

    def og_rows(h):
        return (0, width) if h is None else ((0, cut), (cut, width - cut))[h]

    def og_gather(op, first, count):
        lanes = pl.ds(first * unit, count * unit)

        def view(k, h):
            top, size = og_rows(h)
            return og_all.at[pl.ds(pl.multiple_of(k * width + top, 16), size), lanes]

        return Gather(
            op, view, lambda h: og_ref.at[pl.ds(*og_rows(h)), lanes],
            lambda count: og_all.at[pl.ds(0, count * width), lanes],
        )

    def act_gather(op, r):
        def at(h):
            size = 2 * unit if h is None else unit
            return pl.ds(2 * unit * r + unit * (h or 0), size)

        return Gather(
            op, lambda k, h: act_all.at[k, at(h), :], lambda h: act_ref.at[at(h), :],
            lambda count: act_all.at[pl.ds(0, count), at(None), :],
        )

    def acts_gather(op, u):
        def view(k, h):
            at = pl.ds(pl.multiple_of(k * part, 16), part)
            if h is None:
                return a_all.at[u, :, at, :]
            return a_all.at[u, pl.ds(h * half_planes, half_planes), at, :]

        return Gather(op, view, lambda h: view(j, h), lambda count: a_all.at[u, :, pl.ds(0, count * part), :])

    og = [og_gather(n, *piece) for n, piece in enumerate(pieces)]
    act = [act_gather(len(og) + r, r) for r in range(pairs)]
    acts = [acts_gather(len(og) + len(act) + u, u) for u in range(units)]

    def scale_all():
        csum[...] = jnp.zeros_like(csum)
        loads[2].wait()
        loads[3].wait()
        step_rows = 16

        def scale(i, carry):
            at = pl.ds(pl.multiple_of(i * step_rows, step_rows), step_rows)
            below = eig[at, :] + damp_ref[0]
            for q in range(queries):
                scaled[q, at, :] = (scaled[q, at, :].astype(f32) / below).astype(bf16)
            return carry

        lax.fori_loop(0, width // step_rows, scale, 0)

    def chain(n, block, sends, recvs, to):
        first, count = pieces[n]
        view = g_all.at[block, pl.ds(first, count)]
        return pltpu.make_async_remote_copy(
            src_ref=view, dst_ref=view, send_sem=sends.at[block], recv_sem=recvs.at[block, n],
            device_id={"dp": to}, device_id_type=MESH,
        )

    def whole(block, sends, recvs):
        return pltpu.make_async_remote_copy(
            src_ref=g_all.at[block], dst_ref=g_all.at[block], send_sem=sends.at[block], recv_sem=recvs.at[block, 0],
            device_id={"dp": lax.rem(z + 1, planes)}, device_id_type=MESH,
        )

    def up(block, n):
        return chain(n, block, up_send, up_recv, lax.rem(z + 1, planes))

    def down(block, n):
        return chain(n, block, dn_send, dn_recv, lax.rem(z + planes - 1, planes))

    def service(level, n):
        @pl.when(z - level >= 0)
        def _():
            up(z - level, n).wait_recv()

        @pl.when((z - level >= 0) & (z < planes - 1))
        def _():
            up(z - level, n).start()

        @pl.when(z + level < planes)
        def _():
            down(z + level, n).wait_recv()

        @pl.when((z + level < planes) & (z > 0))
        def _():
            down(z + level, n).start()

    k_tile = 6 * unit
    k_full = depth // k_tile

    k_half = members // 2 * width
    k_near, k_next = k_half // k_tile, -(-k_half // k_tile)
    upper = j // (members // 2)

    def deepen(n, lo, hi, offset):
        first, count = pieces[n]
        at, to = pl.ds(first * unit, count * unit), pl.ds(0, count * unit)

        def inner(k, c):
            deep = pl.ds(pl.multiple_of((k + offset) * k_tile, k_tile), k_tile)
            g_acc[:, to] += jnp.dot(out_b[:, deep], og_all[deep, at], preferred_element_type=f32)
            return c

        lax.fori_loop(lo, hi, inner, 0)

    def project_near(n):
        wide = pieces[n][1] * unit
        g_acc[:, pl.ds(0, wide)] = jnp.zeros((width, wide), f32)
        deepen(n, 0, k_near, upper * k_next)

    def project(n):
        first, count = pieces[n]
        wide = count * unit
        at, to = pl.ds(first * unit, wide), pl.ds(0, wide)
        k_rest = depth - k_full * k_tile
        if k_rest:
            g_acc[:, to] += jnp.dot(
                out_b[:, pl.ds(k_full * k_tile, k_rest)], og_all[pl.ds(k_full * k_tile, k_rest), at],
                preferred_element_type=f32,
            )
        deepen(n, 0, k_full - k_near, (1 - upper) * k_near)
        lane = lax.broadcasted_iota(jnp.int32, (1, unit), 1)
        for i in range(count):
            keep = (lane < len_ref[first + i]).astype(f32)
            g_all[z, first + i] = (g_acc[:, pl.ds(i * unit, unit)] * keep).astype(bf16)

        @pl.when(z < planes - 1)
        def _():
            up(z, n).start()

        @pl.when(z > 0)
        def _():
            down(z, n).start()

    def contract(r):
        at = pl.ds(2 * unit * r, 2 * unit)
        a_acc[...] = jnp.zeros_like(a_acc)

        def body(k, carry):
            deep = pl.ds(pl.multiple_of(k * feats, feats), feats)
            a_acc[...] += jnp.dot(act_all[k, at, :], in_b[deep, :], preferred_element_type=f32)
            return carry

        lax.fori_loop(0, members, body, 0)
        for s in range(2):
            a_loc[2 * r + s] = a_acc[pl.ds(s * unit, unit), :].astype(bf16)

    def own_rows(k):
        return pl.ds(pl.multiple_of(k * part, 16), part)

    def spread_to(r, to):
        return pltpu.make_async_remote_copy(
            src_ref=a_loc.at[pl.ds(2 * r, 2), own_rows(to), :],
            dst_ref=a_part.at[r, j], send_sem=xp_send.at[r], recv_sem=xp_recv.at[r],
            device_id={"tensor": to}, device_id_type=MESH,
        )

    def spreads(r, count):
        view = a_part.at[r, pl.ds(0, count)]
        return pltpu.make_async_remote_copy(
            src_ref=view, dst_ref=view, send_sem=xp_send.at[r], recv_sem=xp_recv.at[r],
            device_id={"tensor": jp}, device_id_type=MESH,
        )

    def spread(r):
        for step in range(1, members):
            spread_to(r, lax.rem(j + step, members)).start()
        a_part[r, j] = a_loc[pl.ds(2 * r, 2), own_rows(j), :]

    def lift_to(r, to, g):
        lane = pl.ds(g * cols, cols)
        return pltpu.make_async_remote_copy(
            src_ref=a_part.at[r, to * group + g], dst_ref=a_all.at[pl.ds(2 * r, 2), z, own_rows(j), lane],
            send_sem=xz_send.at[r], recv_sem=xz_recv.at[r], device_id={"dp": to}, device_id_type=MESH,
        )

    def lifts(r):
        view = a_part.at[r, pl.ds(0, (planes - 1) * group)]
        return pltpu.make_async_remote_copy(
            src_ref=view, dst_ref=view, send_sem=xz_send.at[r], recv_sem=xz_recv.at[r],
            device_id={"dp": lax.rem(z + 1, planes)}, device_id_type=MESH,
        )

    def lift(r):
        spreads(r, members - 1).wait_recv()
        for step in range(1, planes):
            for g in range(group):
                lift_to(r, lax.rem(z + step, planes), g).start()
        for g in range(group):
            a_all[pl.ds(2 * r, 2), z, own_rows(j), pl.ds(g * cols, cols)] = a_part[r, z * group + g]

    def lifted(r):
        lifts(r).wait_recv()

    def score(side, *which):
        h = (z // 2 + side) % 2

        def body(i, carry):
            u = which[0] + i
            block = a_all[u, pl.ds(2 * h, 2)].reshape(2 * unit, span)
            for q in range(queries):
                mixed = lax.dot_general(
                    scaled[q], block, (((1,), (1,)), ((), ())), preferred_element_type=f32
                )
                for b in range(2):
                    csum[2 * h + b, u, pl.ds(q, 1), :] = jnp.sum(
                        mixed[:, b * unit:(b + 1) * unit] * g_all[2 * h + b, u].astype(f32), axis=0, keepdims=True
                    )
            return carry

        lax.fori_loop(0, len(which), body, 0)

    def loaded(*which):
        for n in which:
            loads[n].wait()

    meet()
    og[0].begin()
    scale_all()
    og[0].relay()
    og[1].begin()
    og[0].near()
    og[2].begin()
    loaded(0, 4)
    og[0].paired()
    project_near(0)
    og[0].far()
    og[0].finish()
    project(0)
    og[1].relay()
    act[0].begin()
    og[1].near()
    og[1].paired()
    project_near(1)
    service(1, 0)
    og[1].far()
    og[2].relay()
    act[1].begin()
    og[2].near()
    og[1].finish()
    project(1)
    service(2, 0)
    act[0].relay()
    act[2].begin()
    act[0].near()
    og[2].paired()
    project_near(2)
    og[2].far()
    og[2].finish()
    service(1, 1)
    project(2)
    service(3, 0)
    loaded(1, 5)
    service(2, 1)
    act[0].far()
    act[0].paired()
    act[0].finish()
    act[1].relay()
    act[1].near()
    contract(0)
    spread(0)
    service(1, 2)
    act[2].relay()
    act[2].near()
    og[3].open()
    act[1].far()
    act[1].paired()
    act[1].finish()
    contract(1)
    spread(1)
    lift(0)
    act[2].far()
    act[2].paired()
    act[2].finish()
    contract(2)
    spread(2)
    og[3].extend()
    og[3].relay()
    service(2, 2)
    service(3, 1)
    lift(1)
    lift(2)
    lifted(0)
    acts[0].begin()
    acts[1].begin()
    og[3].near()
    og[3].paired()
    project_near(3)
    og[3].far()
    og[3].finish()
    project(3)
    acts[0].relay()
    acts[0].near()
    lifted(1)
    acts[2].begin()
    acts[1].relay()
    acts[1].near()
    acts[3].begin()
    acts[0].far()
    acts[0].paired()
    acts[0].finish()
    score(0, 0)
    acts[2].relay()
    acts[2].near()
    lifted(2)
    acts[4].begin()
    score(1, 0)
    acts[1].far()
    acts[1].paired()
    acts[1].finish()
    score(0, 1)
    service(3, 2)
    acts[3].relay()
    acts[3].near()
    acts[5].begin()
    service(1, 3)
    score(1, 1)
    acts[2].far()
    acts[2].paired()
    acts[2].finish()
    score(0, 2)
    acts[4].relay()
    acts[4].near()
    score(1, 2)
    acts[3].far()
    acts[3].paired()
    acts[3].finish()
    score(0, 3)
    service(2, 3)
    acts[5].relay()
    acts[5].near()
    score(1, 3)
    acts[4].far()
    acts[4].paired()
    acts[4].finish()
    score(0, 4)
    acts[5].far()
    acts[5].paired()
    acts[5].finish()
    score(0, 5)
    service(3, 3)
    score(1, 4, 5)
    per = res_ref.shape[1]
    lane_at = lax.broadcasted_iota(jnp.int32, (8, per), 1)
    for b in range(planes):
        tile = jnp.zeros((8, per), f32)
        for u in range(units):
            total = jnp.sum(csum[b, u], axis=1, keepdims=True)
            tile = tile + jnp.where(lane_at == u, total, 0.0)
        tiles[b] = tile

    def fold(to):
        return pltpu.make_async_remote_copy(
            src_ref=tiles.at[to], dst_ref=got_z.at[z], send_sem=rz_send.at[0], recv_sem=rz_recv.at[0],
            device_id={"dp": to}, device_id_type=MESH,
        )

    def folds():
        view = got_z.at[pl.ds(0, planes - 1)]
        return pltpu.make_async_remote_copy(
            src_ref=view, dst_ref=view, send_sem=rz_send.at[0], recv_sem=rz_recv.at[0],
            device_id={"dp": lax.rem(z + 1, planes)}, device_id_type=MESH,
        )

    def fold_all():
        for step in range(1, planes):
            fold(lax.rem(z + step, planes)).start()
        got_z[z] = tiles[z]
        folds().wait_recv()
        total = got_z[0]
        for b in range(1, planes):
            total = total + got_z[b]
        got_p[j] = total

    def share(to):
        return pltpu.make_async_remote_copy(
            src_ref=got_p.at[j], dst_ref=got_p.at[j], send_sem=rp_send.at[0], recv_sem=rp_recv.at[0],
            device_id={"tensor": to}, device_id_type=MESH,
        )

    def shares():
        view = got_p.at[pl.ds(0, members - 1)]
        return pltpu.make_async_remote_copy(
            src_ref=view, dst_ref=view, send_sem=rp_send.at[0], recv_sem=rp_recv.at[0],
            device_id={"tensor": jp}, device_id_type=MESH,
        )

    def share_all():
        for step in range(1, members):
            share(lax.rem(j + step, members)).start()
        shares().wait_recv()
        total = got_p[0]
        for k in range(1, members):
            total = total + got_p[k]
        res_ref[...] = total

    def drain_all():
        for op in og + act + acts:
            op.drain()
        for level in range(planes):
            @pl.when((z - level >= 0) & (z < planes - 1))
            def _():
                whole(z - level, up_send, up_recv).wait_send()

            @pl.when((z + level < planes) & (z > 0))
            def _():
                whole(z + level, dn_send, dn_recv).wait_send()
        for r in range(pairs):
            spreads(r, members - 1).wait_send()
            lifts(r).wait_send()
        folds().wait_send()
        shares().wait_send()

    fold_all()
    share_all()
    drain_all()


def fits(planes, members, activations, out_grads_t, in_basis, query_proj, seq_count):
    rows, feats = activations.shape
    width, tokens = out_grads_t.shape
    cols, span = in_basis.shape[1], query_proj.shape[2]
    unit = rows // seq_count
    return (
        members == 8 and planes == 4 and rows == tokens and rows == unit * seq_count and unit == 16 * members
        and seq_count == 6 and feats % 128 == 0 and cols % 128 == 0 and span % cols == 0 and span == 2 * cols
        and (members * width) // (6 * unit) == members // 2 * width // (6 * unit) - (-(members // 2) * width // (6 * unit))
        and width % 16 == 0 and width > 32 and query_proj.shape[0] <= 8
    )


def local(planes, members, activations, out_grads_t, in_basis, out_basis_t, query_proj, eigvals, damping, lengths):
    seq_count = lengths.shape[0]
    if not fits(planes, members, activations, out_grads_t, in_basis, query_proj, seq_count):
        return generic(activations, out_grads_t, in_basis, out_basis_t, query_proj, eigvals, damping, lengths)
    bf16, f32 = jnp.bfloat16, jnp.float32
    rows, feats = activations.shape
    width, tokens = out_grads_t.shape
    features, cols = in_basis.shape
    depth = out_basis_t.shape[1]
    queries, _, span = query_proj.shape
    unit = rows // seq_count
    part, pairs, group = unit // members, seq_count // 2, span // cols
    pieces = pairs + 1
    ops = pieces + pairs + seq_count
    any_space = pl.BlockSpec(memory_space=pl.ANY)
    vmem = pl.BlockSpec(memory_space=pltpu.VMEM)
    smem = pl.BlockSpec(memory_space=pltpu.SMEM)
    dma = pltpu.SemaphoreType.DMA
    res = pl.pallas_call(
        kernel,
        out_shape=jax.ShapeDtypeStruct((8, 128), f32),
        in_specs=[any_space] * 6 + [smem, smem],
        out_specs=vmem,
        scratch_shapes=[
            pltpu.VMEM((members * width, tokens), bf16),
            pltpu.VMEM((members, rows, feats), bf16),
            pltpu.VMEM((features, cols), bf16),
            pltpu.VMEM((width, depth), bf16),
            pltpu.VMEM((queries, width, span), bf16),
            pltpu.VMEM((width, span), f32),
            pltpu.VMEM((seq_count, planes, unit, span), bf16),
            pltpu.VMEM((pairs, members, 2, part, cols), bf16),
            pltpu.VMEM((seq_count, unit, cols), bf16),
            pltpu.VMEM((2 * unit, cols), f32),
            pltpu.VMEM((planes, seq_count, width, unit), bf16),
            pltpu.VMEM((width, 2 * unit), f32),
            pltpu.VMEM((planes, seq_count, 8, unit), f32),
            pltpu.VMEM((planes, 8, 128), f32),
            pltpu.VMEM((planes, 8, 128), f32),
            pltpu.VMEM((members, 8, 128), f32),
            dma((6,)), dma((ops,)), dma((ops, 6)),
            dma((planes,)), dma((planes, pieces)), dma((planes,)), dma((planes, pieces)),
            dma((pairs,)), dma((pairs,)), dma((pairs,)), dma((pairs,)),
            dma((1,)), dma((1,)), dma((1,)), dma((1,)),
        ],
        compiler_params=pltpu.CompilerParams(
            collective_id=0, has_side_effects=True, vmem_limit_bytes=63 * 1024 * 1024
        ),
    )(activations, out_grads_t, in_basis, out_basis_t, query_proj, eigvals, lengths, damping)
    norm_factor = (features * depth * unit) ** (-0.5)
    return res[:queries, :seq_count].T * norm_factor


def solution(mesh):
    placed = (
        P("dp", "tensor"),
        P("tensor", "dp"),
        P(None, "tensor"),
        P("tensor", None),
        P(None, "tensor", "dp"),
        P("tensor", "dp"),
        P(),
        P("dp"),
    )
    return jax.shard_map(
        functools.partial(local, mesh.shape["dp"], mesh.shape["tensor"]), mesh=mesh, in_specs=placed, out_specs=P("dp", None), check_vma=False
    )
```

```python
import functools

import jax
import jax.numpy as jnp
from jax import lax
from jax.experimental import pallas as pl
from jax.experimental.pallas import tpu as pltpu
from jax.sharding import PartitionSpec as P


def generic(activations, out_grads_t, in_basis, out_basis_t, query_proj, eigvals, damping, lengths):
    bf16, f32 = jnp.bfloat16, jnp.float32
    seq_count = lengths.shape[0]
    full_act = lax.all_gather(activations, "tensor", axis=1, tiled=True)
    token_rows = full_act.shape[0]
    seq_len = token_rows // seq_count
    act_local = jnp.dot(full_act, in_basis, preferred_element_type=f32).astype(bf16)
    act_full = lax.all_gather(act_local, "tensor", axis=1, tiled=True)
    features = act_full.shape[1]
    act_proj = lax.all_to_all(act_full, "dp", split_axis=1, concat_axis=0, tiled=True)
    grad_full = jnp.dot(
        out_basis_t, lax.all_gather(out_grads_t, "tensor", axis=0, tiled=True), preferred_element_type=f32
    )
    position = lax.broadcasted_iota(jnp.int32, (seq_count, seq_len), 1)
    keep = (position < lengths[:, None]).astype(f32).reshape(1, token_rows)
    grad_local = (grad_full * keep).astype(bf16)
    grad_proj = lax.all_gather(grad_local, "dp", axis=1, tiled=True)
    scaled = (query_proj.astype(f32) / (eigvals + damping[0])).astype(bf16)
    mixed = jnp.einsum("td,qjd->qjt", act_proj, scaled, preferred_element_type=f32)
    weighted = mixed * grad_proj.astype(f32)[None, :, :]
    query_count, width, tokens = weighted.shape
    partial_value = jnp.sum(weighted.reshape(query_count, width, tokens // seq_len, seq_len), axis=(1, 3)).T
    totals = lax.psum(partial_value, ("dp", "tensor"))
    mine = lax.dynamic_slice_in_dim(totals, lax.axis_index("dp") * seq_count, seq_count, 0)
    norm_factor = (features * out_basis_t.shape[1] * seq_len) ** (-0.5)
    return mine * norm_factor


MESH = pl.DeviceIdType.MESH


def kernel(
    act_ref, og_ref, in_ref, out_ref, query_ref, eig_ref, len_ref, damp_ref, res_ref,
    og_all, act_all, in_b, out_b, scaled, eig, a_all, a_part, a_loc, a_acc, g_all, g_acc, csum, tiles, got_z, got_p,
    load_sem, gs_send, gs_recv, up_send, dn_send, ch_recv, xp_send, xp_recv, xz_send, xz_recv,
    rz_send, rz_recv, rp_send, rp_recv,
):
    bf16, f32 = jnp.bfloat16, jnp.float32
    z, j = lax.axis_index("dp"), lax.axis_index("tensor")
    members, rows, feats = act_all.shape
    planes, units, width, unit = g_all.shape
    depth = out_b.shape[1]
    queries, span = scaled.shape[0], scaled.shape[2]
    cols = a_loc.shape[2]
    part = unit // members
    pairs = units // 2
    group = span // cols
    half_planes = planes // 2
    pieces = [(0, 1), (1, 1)] + [(2 * n, 2) for n in range(1, pairs)]
    hops = pieces[:-1] + [(units - 2, 1), (units - 1, 1)]
    jx = j + 2 - 4 * lax.rem(j // 2, 2)
    jy = j + 4 - 8 * (j // 4)
    jd = jx + 4 - 8 * (j // 4)

    def mate(k):
        return k + 1 - 2 * lax.rem(k, 2)

    jp = mate(j)

    loads = [
        pltpu.make_async_copy(og_ref, og_all.at[pl.ds(pl.multiple_of(j * width, 16), width), :], load_sem.at[0]),
        pltpu.make_async_copy(act_ref, act_all.at[j], load_sem.at[1]),
        pltpu.make_async_copy(query_ref, scaled, load_sem.at[2]),
        pltpu.make_async_copy(eig_ref, eig, load_sem.at[3]),
        pltpu.make_async_copy(out_ref, out_b, load_sem.at[4]),
        pltpu.make_async_copy(in_ref, in_b, load_sem.at[5]),
    ]
    for load in loads:
        load.start()

    barrier = pltpu.get_barrier_semaphore()
    for step in range(1, members):
        pl.semaphore_signal(barrier, inc=1, device_id={"tensor": lax.rem(j + step, members)}, device_id_type=MESH)
    for step in range(1, planes):
        pl.semaphore_signal(barrier, inc=1, device_id={"dp": lax.rem(z + step, planes)}, device_id_type=MESH)

    def meet():
        pl.semaphore_wait(barrier, members + planes - 2)

    class Gather:
        def __init__(self, op, view, own, several):
            self.op, self.view, self.own, self.several = op, view, own, several
            self.plan = [
                (j, 0, jx), (j, 1, jx), (jy, 1, jx),
                (j, 1, jy), (j, 0, jy), (jx, 0, jy),
                (j, None, jp), (jx, None, jp), (jy, None, jp), (jd, 0, jp), (jd, 1, jp),
            ]
            self.lane = (0, 2, 3, 1, 2, 3, 4, 4, 4, 5, 5)

        def copy(self, slot):
            block, half, target = self.plan[slot]
            src = self.own(half) if slot in (0, 1, 3, 4, 6) else self.view(block, half)
            return pltpu.make_async_remote_copy(
                src_ref=src, dst_ref=self.view(block, half), send_sem=gs_send.at[self.op],
                recv_sem=gs_recv.at[self.op, self.lane[slot]], device_id={"tensor": target}, device_id_type=MESH,
            )

        def start(self, *slots):
            for slot in slots:
                self.copy(slot).start()

        def arrive(self, lane, view):
            pltpu.make_async_remote_copy(
                src_ref=view, dst_ref=view, send_sem=gs_send.at[self.op],
                recv_sem=gs_recv.at[self.op, lane], device_id={"tensor": jp}, device_id_type=MESH,
            ).wait_recv()

        def begin(self):
            self.start(0, 3, 1, 4, 6)

        def open(self):
            self.start(0, 3)

        def extend(self):
            self.start(1, 4, 6)

        def relay(self):
            self.arrive(0, self.view(jx, 0))
            self.start(5)
            self.arrive(1, self.view(jy, 1))
            self.start(2)

        def near(self):
            self.arrive(2, self.view(jx, None))
            self.start(7, 8)

        def far(self):
            self.arrive(3, self.view(jd, None))
            self.start(9, 10)

        def paired(self):
            self.arrive(4, self.several(3))

        def finish(self):
            self.arrive(5, self.view(mate(jd), None))

        def drain(self):
            view = self.several(len(self.plan) - 4)
            pltpu.make_async_remote_copy(
                src_ref=view, dst_ref=view, send_sem=gs_send.at[self.op],
                recv_sem=gs_recv.at[self.op, 0], device_id={"tensor": jp}, device_id_type=MESH,
            ).wait_send()

    cut = (width // 2 + 15) // 16 * 16

    def og_rows(h):
        return (0, width) if h is None else ((0, cut), (cut, width - cut))[h]

    def og_gather(op, first, count):
        lanes = pl.ds(first * unit, count * unit)

        def view(k, h):
            top, size = og_rows(h)
            return og_all.at[pl.ds(pl.multiple_of(k * width + top, 16), size), lanes]

        return Gather(
            op, view, lambda h: og_ref.at[pl.ds(*og_rows(h)), lanes],
            lambda count: og_all.at[pl.ds(0, count * width), lanes],
        )

    def act_gather(op, r):
        def at(h):
            size = 2 * unit if h is None else unit
            return pl.ds(2 * unit * r + unit * (h or 0), size)

        return Gather(
            op, lambda k, h: act_all.at[k, at(h), :], lambda h: act_ref.at[at(h), :],
            lambda count: act_all.at[pl.ds(0, count), at(None), :],
        )

    def acts_gather(op, u):
        def view(k, h):
            at = pl.ds(pl.multiple_of(k * part, 16), part)
            if h is None:
                return a_all.at[u, :, at, :]
            return a_all.at[u, pl.ds(h * half_planes, half_planes), at, :]

        return Gather(op, view, lambda h: view(j, h), lambda count: a_all.at[u, :, pl.ds(0, count * part), :])

    og = [og_gather(n, *piece) for n, piece in enumerate(pieces)]
    act = [act_gather(len(og) + r, r) for r in range(pairs)]
    acts = [acts_gather(u if u < pairs else len(og) + u - pairs, u) for u in range(units)]

    def scale_all():
        csum[...] = jnp.zeros_like(csum)
        loads[2].wait()
        loads[3].wait()
        step_rows = 16

        def scale(i, carry):
            at = pl.ds(pl.multiple_of(i * step_rows, step_rows), step_rows)
            below = eig[at, :] + damp_ref[0]
            for q in range(queries):
                scaled[q, at, :] = (scaled[q, at, :].astype(f32) / below).astype(bf16)
            return carry

        lax.fori_loop(0, width // step_rows, scale, 0)

    def chain(n, block, sends, recvs, to):
        first, count = hops[n]
        view = g_all.at[block, pl.ds(first, count)]
        return pltpu.make_async_remote_copy(
            src_ref=view, dst_ref=view, send_sem=sends.at[block], recv_sem=recvs.at[block, n],
            device_id={"dp": to}, device_id_type=MESH,
        )

    def whole(block, sends, recvs):
        return pltpu.make_async_remote_copy(
            src_ref=g_all.at[block], dst_ref=g_all.at[block], send_sem=sends.at[block], recv_sem=recvs.at[block, 0],
            device_id={"dp": lax.rem(z + 1, planes)}, device_id_type=MESH,
        )

    def up(block, n):
        return chain(n, block, up_send, ch_recv, lax.rem(z + 1, planes))

    def down(block, n):
        return chain(n, block, dn_send, ch_recv, lax.rem(z + planes - 1, planes))

    def service(level, n):
        @pl.when(z - level >= 0)
        def _():
            up(z - level, n).wait_recv()

        @pl.when((z - level >= 0) & (z < planes - 1))
        def _():
            up(z - level, n).start()

        @pl.when(z + level < planes)
        def _():
            down(z + level, n).wait_recv()

        @pl.when((z + level < planes) & (z > 0))
        def _():
            down(z + level, n).start()

    k_tile = 6 * unit
    k_full = depth // k_tile

    k_half = members // 2 * width
    k_near, k_next = k_half // k_tile, -(-k_half // k_tile)
    upper = j // (members // 2)

    def deepen(n, lo, hi, offset):
        first, count = pieces[n]
        at, to = pl.ds(first * unit, count * unit), pl.ds(0, count * unit)

        def inner(k, c):
            deep = pl.ds(pl.multiple_of((k + offset) * k_tile, k_tile), k_tile)
            g_acc[:, to] += jnp.dot(out_b[:, deep], og_all[deep, at], preferred_element_type=f32)
            return c

        lax.fori_loop(lo, hi, inner, 0)

    def project_near(n):
        wide = pieces[n][1] * unit
        g_acc[:, pl.ds(0, wide)] = jnp.zeros((width, wide), f32)
        deepen(n, 0, k_near, upper * k_next)

    def project(n):
        first, count = pieces[n]
        wide = count * unit
        at, to = pl.ds(first * unit, wide), pl.ds(0, wide)
        k_rest = depth - k_full * k_tile
        if k_rest:
            g_acc[:, to] += jnp.dot(
                out_b[:, pl.ds(k_full * k_tile, k_rest)], og_all[pl.ds(k_full * k_tile, k_rest), at],
                preferred_element_type=f32,
            )
        deepen(n, 0, k_full - k_near, (1 - upper) * k_near)
        lane = lax.broadcasted_iota(jnp.int32, (1, unit), 1)
        for hop in range(n, n + 1 if n < len(pieces) - 1 else len(hops)):
            for i in range(hops[hop][0], sum(hops[hop])):
                keep = (lane < len_ref[i]).astype(f32)
                g_all[z, i] = (g_acc[:, pl.ds((i - first) * unit, unit)] * keep).astype(bf16)

            @pl.when(z < planes - 1)
            def _():
                up(z, hop).start()

            @pl.when(z > 0)
            def _():
                down(z, hop).start()

    def contract(r):
        at = pl.ds(2 * unit * r, 2 * unit)
        a_acc[...] = jnp.zeros_like(a_acc)

        def body(k, carry):
            deep = pl.ds(pl.multiple_of(k * feats, feats), feats)
            a_acc[...] += jnp.dot(act_all[k, at, :], in_b[deep, :], preferred_element_type=f32)
            return carry

        lax.fori_loop(0, members, body, 0)
        for s in range(2):
            a_loc[2 * r + s] = a_acc[pl.ds(s * unit, unit), :].astype(bf16)

    def own_rows(k):
        return pl.ds(pl.multiple_of(k * part, 16), part)

    def spread_to(r, to):
        return pltpu.make_async_remote_copy(
            src_ref=a_loc.at[pl.ds(2 * r, 2), own_rows(to), :],
            dst_ref=a_part.at[r, j], send_sem=xp_send.at[r], recv_sem=xp_recv.at[r],
            device_id={"tensor": to}, device_id_type=MESH,
        )

    def spreads(r, count):
        view = a_part.at[r, pl.ds(0, count)]
        return pltpu.make_async_remote_copy(
            src_ref=view, dst_ref=view, send_sem=xp_send.at[r], recv_sem=xp_recv.at[r],
            device_id={"tensor": jp}, device_id_type=MESH,
        )

    def spread(r):
        for step in range(1, members):
            spread_to(r, lax.rem(j + step, members)).start()
        a_part[r, j] = a_loc[pl.ds(2 * r, 2), own_rows(j), :]

    def lift_to(r, to, g):
        lane = pl.ds(g * cols, cols)
        return pltpu.make_async_remote_copy(
            src_ref=a_part.at[r, to * group + g], dst_ref=a_all.at[pl.ds(2 * r, 2), z, own_rows(j), lane],
            send_sem=xz_send.at[r], recv_sem=xz_recv.at[r], device_id={"dp": to}, device_id_type=MESH,
        )

    def lifts(r):
        view = a_part.at[r, pl.ds(0, (planes - 1) * group)]
        return pltpu.make_async_remote_copy(
            src_ref=view, dst_ref=view, send_sem=xz_send.at[r], recv_sem=xz_recv.at[r],
            device_id={"dp": lax.rem(z + 1, planes)}, device_id_type=MESH,
        )

    def lift(r):
        spreads(r, members - 1).wait_recv()
        for step in range(1, planes):
            for g in range(group):
                lift_to(r, lax.rem(z + step, planes), g).start()
        for g in range(group):
            a_all[pl.ds(2 * r, 2), z, own_rows(j), pl.ds(g * cols, cols)] = a_part[r, z * group + g]

    def lifted(r):
        lifts(r).wait_recv()

    def score(side, *which):
        h = (z // 2 + side) % 2

        def body(i, carry):
            u = which[0] + i
            block = a_all[u, pl.ds(2 * h, 2)].reshape(2 * unit, span)
            for q in range(queries):
                mixed = lax.dot_general(
                    scaled[q], block, (((1,), (1,)), ((), ())), preferred_element_type=f32
                )
                for b in range(2):
                    csum[2 * h + b, u, pl.ds(q, 1), :] = jnp.sum(
                        mixed[:, b * unit:(b + 1) * unit] * g_all[2 * h + b, u].astype(f32), axis=0, keepdims=True
                    )
            return carry

        lax.fori_loop(0, len(which), body, 0)

    def loaded(*which):
        for n in which:
            loads[n].wait()

    meet()
    og[0].begin()
    scale_all()
    og[0].relay()
    og[1].begin()
    og[0].near()
    og[2].begin()
    loaded(0, 4)
    og[0].paired()
    project_near(0)
    og[0].far()
    og[0].finish()
    project(0)
    og[1].relay()
    act[0].begin()
    og[1].near()
    og[1].paired()
    project_near(1)
    service(1, 0)
    og[1].far()
    og[2].relay()
    act[1].begin()
    og[2].near()
    og[1].finish()
    project(1)
    service(2, 0)
    act[0].relay()
    act[2].begin()
    act[0].near()
    og[2].paired()
    project_near(2)
    og[2].far()
    og[2].finish()
    service(1, 1)
    project(2)
    service(3, 0)
    loaded(1, 5)
    service(2, 1)
    act[0].far()
    act[0].paired()
    act[0].finish()
    act[1].relay()
    act[1].near()
    contract(0)
    spread(0)
    service(1, 2)
    act[2].relay()
    act[2].near()
    og[3].open()
    act[1].far()
    act[1].paired()
    act[1].finish()
    contract(1)
    spread(1)
    lift(0)
    act[2].far()
    act[2].paired()
    act[2].finish()
    contract(2)
    spread(2)
    og[3].extend()
    og[3].relay()
    service(2, 2)
    service(3, 1)
    lift(1)
    lift(2)
    lifted(0)
    og[0].drain()
    acts[0].begin()
    og[1].drain()
    acts[1].begin()
    og[3].near()
    og[3].paired()
    project_near(3)
    og[3].far()
    og[3].finish()
    project(3)
    acts[0].relay()
    acts[0].near()
    lifted(1)
    og[2].drain()
    acts[2].begin()
    acts[1].relay()
    act[0].drain()
    acts[3].begin()
    acts[1].near()
    acts[0].far()
    acts[0].paired()
    acts[0].finish()
    score(0, 0)
    acts[2].relay()
    acts[2].near()
    lifted(2)
    act[1].drain()
    acts[4].begin()
    acts[1].far()
    score(1, 0)
    service(1, 3)
    acts[1].paired()
    acts[1].finish()
    score(0, 1)
    acts[3].relay()
    acts[3].near()
    act[2].drain()
    acts[5].begin()
    acts[2].far()
    service(1, 4)
    score(1, 1)
    acts[2].paired()
    acts[2].finish()
    score(0, 2)
    acts[4].relay()
    acts[4].near()
    acts[3].far()
    service(3, 2)
    score(1, 2)
    service(2, 3)
    acts[3].paired()
    acts[3].finish()
    score(0, 3)
    acts[5].relay()
    acts[5].near()
    acts[4].far()
    service(2, 4)
    score(1, 3)
    acts[4].paired()
    acts[4].finish()
    score(0, 4)
    acts[5].far()
    service(3, 3)
    score(1, 4)
    acts[5].paired()
    acts[5].finish()
    score(0, 5)
    service(3, 4)
    score(1, 5)
    per = res_ref.shape[1]
    lane_at = lax.broadcasted_iota(jnp.int32, (8, per), 1)
    for b in range(planes):
        tile = jnp.zeros((8, per), f32)
        for u in range(units):
            total = jnp.sum(csum[b, u], axis=1, keepdims=True)
            tile = tile + jnp.where(lane_at == u, total, 0.0)
        tiles[b] = tile

    def fold(to):
        return pltpu.make_async_remote_copy(
            src_ref=tiles.at[to], dst_ref=got_z.at[z], send_sem=rz_send.at[0], recv_sem=rz_recv.at[0],
            device_id={"dp": to}, device_id_type=MESH,
        )

    def folds():
        view = got_z.at[pl.ds(0, planes - 1)]
        return pltpu.make_async_remote_copy(
            src_ref=view, dst_ref=view, send_sem=rz_send.at[0], recv_sem=rz_recv.at[0],
            device_id={"dp": lax.rem(z + 1, planes)}, device_id_type=MESH,
        )

    def fold_all():
        for step in range(1, planes):
            fold(lax.rem(z + step, planes)).start()
        got_z[z] = tiles[z]
        folds().wait_recv()
        total = got_z[0]
        for b in range(1, planes):
            total = total + got_z[b]
        got_p[j] = total

    def share(to):
        return pltpu.make_async_remote_copy(
            src_ref=got_p.at[j], dst_ref=got_p.at[j], send_sem=rp_send.at[0], recv_sem=rp_recv.at[0],
            device_id={"tensor": to}, device_id_type=MESH,
        )

    def shares():
        view = got_p.at[pl.ds(0, members - 1)]
        return pltpu.make_async_remote_copy(
            src_ref=view, dst_ref=view, send_sem=rp_send.at[0], recv_sem=rp_recv.at[0],
            device_id={"tensor": jp}, device_id_type=MESH,
        )

    def share_all():
        for step in range(1, members):
            share(lax.rem(j + step, members)).start()
        shares().wait_recv()
        total = got_p[0]
        for k in range(1, members):
            total = total + got_p[k]
        res_ref[...] = total

    def drain_all():
        for op in og[pairs:] + acts:
            op.drain()
        for level in range(planes):
            @pl.when((z - level >= 0) & (z < planes - 1))
            def _():
                whole(z - level, up_send, ch_recv).wait_send()

            @pl.when((z + level < planes) & (z > 0))
            def _():
                whole(z + level, dn_send, ch_recv).wait_send()
        for r in range(pairs):
            spreads(r, members - 1).wait_send()
            lifts(r).wait_send()
        folds().wait_send()
        shares().wait_send()

    fold_all()
    share_all()
    drain_all()


def fits(planes, members, activations, out_grads_t, in_basis, query_proj, seq_count):
    rows, feats = activations.shape
    width, tokens = out_grads_t.shape
    cols, span = in_basis.shape[1], query_proj.shape[2]
    unit = rows // seq_count
    return (
        members == 8 and planes == 4 and rows == tokens and rows == unit * seq_count and unit == 16 * members
        and seq_count == 6 and feats % 128 == 0 and cols % 128 == 0 and span % cols == 0 and span == 2 * cols
        and (members * width) // (6 * unit) == members // 2 * width // (6 * unit) - (-(members // 2) * width // (6 * unit))
        and width % 16 == 0 and width > 32 and query_proj.shape[0] <= 8
    )


def local(planes, members, activations, out_grads_t, in_basis, out_basis_t, query_proj, eigvals, damping, lengths):
    seq_count = lengths.shape[0]
    if not fits(planes, members, activations, out_grads_t, in_basis, query_proj, seq_count):
        return generic(activations, out_grads_t, in_basis, out_basis_t, query_proj, eigvals, damping, lengths)
    bf16, f32 = jnp.bfloat16, jnp.float32
    rows, feats = activations.shape
    width, tokens = out_grads_t.shape
    features, cols = in_basis.shape
    depth = out_basis_t.shape[1]
    queries, _, span = query_proj.shape
    unit = rows // seq_count
    part, pairs, group = unit // members, seq_count // 2, span // cols
    pieces = pairs + 1
    ops = pieces + pairs
    any_space = pl.BlockSpec(memory_space=pl.ANY)
    vmem = pl.BlockSpec(memory_space=pltpu.VMEM)
    smem = pl.BlockSpec(memory_space=pltpu.SMEM)
    dma = pltpu.SemaphoreType.DMA
    res = pl.pallas_call(
        kernel,
        out_shape=jax.ShapeDtypeStruct((8, 128), f32),
        in_specs=[any_space] * 6 + [smem, smem],
        out_specs=vmem,
        scratch_shapes=[
            pltpu.VMEM((members * width, tokens), bf16),
            pltpu.VMEM((members, rows, feats), bf16),
            pltpu.VMEM((features, cols), bf16),
            pltpu.VMEM((width, depth), bf16),
            pltpu.VMEM((queries, width, span), bf16),
            pltpu.VMEM((width, span), f32),
            pltpu.VMEM((seq_count, planes, unit, span), bf16),
            pltpu.VMEM((pairs, members, 2, part, cols), bf16),
            pltpu.VMEM((seq_count, unit, cols), bf16),
            pltpu.VMEM((2 * unit, cols), f32),
            pltpu.VMEM((planes, seq_count, width, unit), bf16),
            pltpu.VMEM((width, 2 * unit), f32),
            pltpu.VMEM((planes, seq_count, 8, unit), f32),
            pltpu.VMEM((planes, 8, 128), f32),
            pltpu.VMEM((planes, 8, 128), f32),
            pltpu.VMEM((members, 8, 128), f32),
            dma((6,)), dma((ops,)), dma((ops, 6)),
            dma((planes,)), dma((planes,)), dma((planes, pieces + 1)),
            dma((pairs,)), dma((pairs,)), dma((pairs,)), dma((pairs,)),
            dma((1,)), dma((1,)), dma((1,)), dma((1,)),
        ],
        compiler_params=pltpu.CompilerParams(
            collective_id=0, has_side_effects=True, vmem_limit_bytes=63 * 1024 * 1024
        ),
    )(activations, out_grads_t, in_basis, out_basis_t, query_proj, eigvals, lengths, damping)
    norm_factor = (features * depth * unit) ** (-0.5)
    return res[:queries, :seq_count].T * norm_factor


def solution(mesh):
    placed = (
        P("dp", "tensor"),
        P("tensor", "dp"),
        P(None, "tensor"),
        P("tensor", None),
        P(None, "tensor", "dp"),
        P("tensor", "dp"),
        P(),
        P("dp"),
    )
    return jax.shard_map(
        functools.partial(local, mesh.shape["dp"], mesh.shape["tensor"]), mesh=mesh, in_specs=placed, out_specs=P("dp", None), check_vma=False
    )
```

```python
import functools

import jax
import jax.numpy as jnp
from jax import lax
from jax.experimental import pallas as pl
from jax.experimental.pallas import tpu as pltpu
from jax.sharding import PartitionSpec as P


def generic(activations, out_grads_t, in_basis, out_basis_t, query_proj, eigvals, damping, lengths):
    bf16, f32 = jnp.bfloat16, jnp.float32
    seq_count = lengths.shape[0]
    full_act = lax.all_gather(activations, "tensor", axis=1, tiled=True)
    token_rows = full_act.shape[0]
    seq_len = token_rows // seq_count
    act_local = jnp.dot(full_act, in_basis, preferred_element_type=f32).astype(bf16)
    act_full = lax.all_gather(act_local, "tensor", axis=1, tiled=True)
    features = act_full.shape[1]
    act_proj = lax.all_to_all(act_full, "dp", split_axis=1, concat_axis=0, tiled=True)
    grad_full = jnp.dot(
        out_basis_t, lax.all_gather(out_grads_t, "tensor", axis=0, tiled=True), preferred_element_type=f32
    )
    position = lax.broadcasted_iota(jnp.int32, (seq_count, seq_len), 1)
    keep = (position < lengths[:, None]).astype(f32).reshape(1, token_rows)
    grad_local = (grad_full * keep).astype(bf16)
    grad_proj = lax.all_gather(grad_local, "dp", axis=1, tiled=True)
    scaled = (query_proj.astype(f32) / (eigvals + damping[0])).astype(bf16)
    mixed = jnp.einsum("td,qjd->qjt", act_proj, scaled, preferred_element_type=f32)
    weighted = mixed * grad_proj.astype(f32)[None, :, :]
    query_count, width, tokens = weighted.shape
    partial_value = jnp.sum(weighted.reshape(query_count, width, tokens // seq_len, seq_len), axis=(1, 3)).T
    totals = lax.psum(partial_value, ("dp", "tensor"))
    mine = lax.dynamic_slice_in_dim(totals, lax.axis_index("dp") * seq_count, seq_count, 0)
    norm_factor = (features * out_basis_t.shape[1] * seq_len) ** (-0.5)
    return mine * norm_factor


MESH = pl.DeviceIdType.MESH


def kernel(
    act_ref, og_ref, in_ref, out_ref, query_ref, eig_ref, len_ref, damp_ref, res_ref,
    og_all, act_all, in_b, out_b, scaled, eig, a_all, a_part, a_loc, a_acc, g_all, g_acc, csum, tiles, got_z, got_p,
    load_sem, gs_send, gs_recv, up_send, dn_send, ch_recv, xp_send, xp_recv, xz_send, xz_recv,
    rz_send, rz_recv, rp_send, rp_recv,
):
    bf16, f32 = jnp.bfloat16, jnp.float32
    z, j = lax.axis_index("dp"), lax.axis_index("tensor")
    members, rows, feats = act_all.shape
    planes, units, width, unit = g_all.shape
    depth = out_b.shape[1]
    queries, span = scaled.shape[0], scaled.shape[2]
    cols = a_loc.shape[2]
    part = unit // members
    pairs = units // 2
    group = span // cols
    half_planes = planes // 2
    pieces = [(0, 1), (1, 1)] + [(2 * n, 2) for n in range(1, pairs)]
    hops = pieces[:-1] + [(units - 2, 1), (units - 1, 1)]
    jx = j + 2 - 4 * lax.rem(j // 2, 2)
    jy = j + 4 - 8 * (j // 4)
    jd = jx + 4 - 8 * (j // 4)

    def mate(k):
        return k + 1 - 2 * lax.rem(k, 2)

    jp = mate(j)

    loads = [
        pltpu.make_async_copy(og_ref, og_all.at[pl.ds(pl.multiple_of(j * width, 16), width), :], load_sem.at[0]),
        pltpu.make_async_copy(act_ref, act_all.at[j], load_sem.at[1]),
        pltpu.make_async_copy(query_ref, scaled, load_sem.at[2]),
        pltpu.make_async_copy(eig_ref, eig, load_sem.at[3]),
        pltpu.make_async_copy(out_ref, out_b, load_sem.at[4]),
        pltpu.make_async_copy(in_ref, in_b, load_sem.at[5]),
    ]
    for load in loads:
        load.start()

    barrier = pltpu.get_barrier_semaphore()
    for step in range(1, members):
        pl.semaphore_signal(barrier, inc=1, device_id={"tensor": lax.rem(j + step, members)}, device_id_type=MESH)
    for step in range(1, planes):
        pl.semaphore_signal(barrier, inc=1, device_id={"dp": lax.rem(z + step, planes)}, device_id_type=MESH)

    def meet():
        pl.semaphore_wait(barrier, members + planes - 2)

    class Gather:
        def __init__(self, op, view, own, several):
            self.op, self.view, self.own, self.several = op, view, own, several
            self.plan = [
                (j, 0, jx), (j, 1, jx), (jy, 1, jx),
                (j, 1, jy), (j, 0, jy), (jx, 0, jy),
                (j, None, jp), (jx, None, jp), (jy, None, jp), (jd, 0, jp), (jd, 1, jp),
            ]
            self.lane = (0, 2, 3, 1, 2, 3, 4, 4, 4, 5, 5)

        def copy(self, slot):
            block, half, target = self.plan[slot]
            src = self.own(half) if slot in (0, 1, 3, 4, 6) else self.view(block, half)
            return pltpu.make_async_remote_copy(
                src_ref=src, dst_ref=self.view(block, half), send_sem=gs_send.at[self.op],
                recv_sem=gs_recv.at[self.op, self.lane[slot]], device_id={"tensor": target}, device_id_type=MESH,
            )

        def start(self, *slots):
            for slot in slots:
                self.copy(slot).start()

        def arrive(self, lane, view):
            pltpu.make_async_remote_copy(
                src_ref=view, dst_ref=view, send_sem=gs_send.at[self.op],
                recv_sem=gs_recv.at[self.op, lane], device_id={"tensor": jp}, device_id_type=MESH,
            ).wait_recv()

        def begin(self):
            self.start(0, 3, 1, 4, 6)

        def open(self):
            self.start(0, 3)

        def extend(self):
            self.start(1, 4, 6)

        def relay(self):
            self.arrive(0, self.view(jx, 0))
            self.start(5)
            self.arrive(1, self.view(jy, 1))
            self.start(2)

        def near(self):
            self.arrive(2, self.view(jx, None))
            self.start(7, 8)

        def far(self):
            self.arrive(3, self.view(jd, None))
            self.start(9, 10)

        def paired(self):
            self.arrive(4, self.several(3))

        def finish(self):
            self.arrive(5, self.view(mate(jd), None))

        def drain(self):
            view = self.several(len(self.plan) - 4)
            pltpu.make_async_remote_copy(
                src_ref=view, dst_ref=view, send_sem=gs_send.at[self.op],
                recv_sem=gs_recv.at[self.op, 0], device_id={"tensor": jp}, device_id_type=MESH,
            ).wait_send()

    cut = (width // 2 + 15) // 16 * 16

    def og_rows(h):
        return (0, width) if h is None else ((0, cut), (cut, width - cut))[h]

    def og_gather(op, first, count):
        lanes = pl.ds(first * unit, count * unit)

        def view(k, h):
            top, size = og_rows(h)
            return og_all.at[pl.ds(pl.multiple_of(k * width + top, 16), size), lanes]

        return Gather(
            op, view, lambda h: og_ref.at[pl.ds(*og_rows(h)), lanes],
            lambda count: og_all.at[pl.ds(0, count * width), lanes],
        )

    def act_gather(op, r):
        def at(h):
            size = 2 * unit if h is None else unit
            return pl.ds(2 * unit * r + unit * (h or 0), size)

        return Gather(
            op, lambda k, h: act_all.at[k, at(h), :], lambda h: act_ref.at[at(h), :],
            lambda count: act_all.at[pl.ds(0, count), at(None), :],
        )

    def acts_gather(op, u):
        def view(k, h):
            at = pl.ds(pl.multiple_of(k * part, 16), part)
            if h is None:
                return a_all.at[u, :, at, :]
            return a_all.at[u, pl.ds(h * half_planes, half_planes), at, :]

        return Gather(op, view, lambda h: view(j, h), lambda count: a_all.at[u, :, pl.ds(0, count * part), :])

    og = [og_gather(n, *piece) for n, piece in enumerate(pieces)]
    act = [act_gather(len(og) + r, r) for r in range(pairs)]
    acts = [acts_gather(u if u < pairs else len(og) + u - pairs, u) for u in range(units)]

    def scale_all():
        csum[...] = jnp.zeros_like(csum)
        loads[2].wait()
        loads[3].wait()
        step_rows = 16

        def scale(i, carry):
            at = pl.ds(pl.multiple_of(i * step_rows, step_rows), step_rows)
            below = eig[at, :] + damp_ref[0]
            for q in range(queries):
                scaled[q, at, :] = (scaled[q, at, :].astype(f32) / below).astype(bf16)
            return carry

        lax.fori_loop(0, width // step_rows, scale, 0)

    def chain(n, block, sends, recvs, to):
        first, count = hops[n]
        view = g_all.at[block, pl.ds(first, count)]
        return pltpu.make_async_remote_copy(
            src_ref=view, dst_ref=view, send_sem=sends.at[block], recv_sem=recvs.at[block, n],
            device_id={"dp": to}, device_id_type=MESH,
        )

    def whole(block, sends, recvs):
        return pltpu.make_async_remote_copy(
            src_ref=g_all.at[block], dst_ref=g_all.at[block], send_sem=sends.at[block], recv_sem=recvs.at[block, 0],
            device_id={"dp": lax.rem(z + 1, planes)}, device_id_type=MESH,
        )

    def up(block, n):
        return chain(n, block, up_send, ch_recv, lax.rem(z + 1, planes))

    def down(block, n):
        return chain(n, block, dn_send, ch_recv, lax.rem(z + planes - 1, planes))

    def service(level, n):
        @pl.when(z - level >= 0)
        def _():
            up(z - level, n).wait_recv()

        @pl.when((z - level >= 0) & (z < planes - 1))
        def _():
            up(z - level, n).start()

        @pl.when(z + level < planes)
        def _():
            down(z + level, n).wait_recv()

        @pl.when((z + level < planes) & (z > 0))
        def _():
            down(z + level, n).start()

    k_tile = 6 * unit
    k_full = depth // k_tile

    k_half = members // 2 * width
    k_near, k_next = k_half // k_tile, -(-k_half // k_tile)
    upper = j // (members // 2)

    def deepen(n, lo, hi, offset):
        first, count = pieces[n]
        at, to = pl.ds(first * unit, count * unit), pl.ds(0, count * unit)

        def inner(k, c):
            deep = pl.ds(pl.multiple_of((k + offset) * k_tile, k_tile), k_tile)
            g_acc[:, to] += jnp.dot(out_b[:, deep], og_all[deep, at], preferred_element_type=f32)
            return c

        lax.fori_loop(lo, hi, inner, 0)

    def project_near(n):
        wide = pieces[n][1] * unit
        g_acc[:, pl.ds(0, wide)] = jnp.zeros((width, wide), f32)
        deepen(n, 0, k_near, upper * k_next)

    def project(n):
        first, count = pieces[n]
        wide = count * unit
        at, to = pl.ds(first * unit, wide), pl.ds(0, wide)
        k_rest = depth - k_full * k_tile
        if k_rest:
            g_acc[:, to] += jnp.dot(
                out_b[:, pl.ds(k_full * k_tile, k_rest)], og_all[pl.ds(k_full * k_tile, k_rest), at],
                preferred_element_type=f32,
            )
        deepen(n, 0, k_full - k_near, (1 - upper) * k_near)
        lane = lax.broadcasted_iota(jnp.int32, (1, unit), 1)
        for hop in range(n, n + 1 if n < len(pieces) - 1 else len(hops)):
            for i in range(hops[hop][0], sum(hops[hop])):
                keep = (lane < len_ref[i]).astype(f32)
                g_all[z, i] = (g_acc[:, pl.ds((i - first) * unit, unit)] * keep).astype(bf16)

            @pl.when(z < planes - 1)
            def _():
                up(z, hop).start()

            @pl.when(z > 0)
            def _():
                down(z, hop).start()

    def contract(r):
        at = pl.ds(2 * unit * r, 2 * unit)
        a_acc[...] = jnp.zeros_like(a_acc)

        def body(k, carry):
            deep = pl.ds(pl.multiple_of(k * feats, feats), feats)
            a_acc[...] += jnp.dot(act_all[k, at, :], in_b[deep, :], preferred_element_type=f32)
            return carry

        lax.fori_loop(0, members, body, 0)
        for s in range(2):
            a_loc[2 * r + s] = a_acc[pl.ds(s * unit, unit), :].astype(bf16)

    def own_rows(k):
        return pl.ds(pl.multiple_of(k * part, 16), part)

    def spread_to(r, to):
        return pltpu.make_async_remote_copy(
            src_ref=a_loc.at[pl.ds(2 * r, 2), own_rows(to), :],
            dst_ref=a_part.at[r, j], send_sem=xp_send.at[r], recv_sem=xp_recv.at[r],
            device_id={"tensor": to}, device_id_type=MESH,
        )

    def spreads(r, count):
        view = a_part.at[r, pl.ds(0, count)]
        return pltpu.make_async_remote_copy(
            src_ref=view, dst_ref=view, send_sem=xp_send.at[r], recv_sem=xp_recv.at[r],
            device_id={"tensor": jp}, device_id_type=MESH,
        )

    def spread(r):
        for step in range(1, members):
            spread_to(r, lax.rem(j + step, members)).start()
        a_part[r, j] = a_loc[pl.ds(2 * r, 2), own_rows(j), :]

    def lift_to(r, to, g):
        lane = pl.ds(g * cols, cols)
        return pltpu.make_async_remote_copy(
            src_ref=a_part.at[r, to * group + g], dst_ref=a_all.at[pl.ds(2 * r, 2), z, own_rows(j), lane],
            send_sem=xz_send.at[r], recv_sem=xz_recv.at[r], device_id={"dp": to}, device_id_type=MESH,
        )

    def lifts(r):
        view = a_part.at[r, pl.ds(0, (planes - 1) * group)]
        return pltpu.make_async_remote_copy(
            src_ref=view, dst_ref=view, send_sem=xz_send.at[r], recv_sem=xz_recv.at[r],
            device_id={"dp": lax.rem(z + 1, planes)}, device_id_type=MESH,
        )

    def lift(r):
        spreads(r, members - 1).wait_recv()
        for step in range(1, planes):
            for g in range(group):
                lift_to(r, lax.rem(z + step, planes), g).start()
        for g in range(group):
            a_all[pl.ds(2 * r, 2), z, own_rows(j), pl.ds(g * cols, cols)] = a_part[r, z * group + g]

    def lifted(r):
        lifts(r).wait_recv()

    def score(side, *which):
        h = (z // 2 + side) % 2

        def body(i, carry):
            u = which[0] + i
            block = a_all[u, pl.ds(2 * h, 2)].reshape(2 * unit, span)
            for q in range(queries):
                mixed = lax.dot_general(
                    scaled[q], block, (((1,), (1,)), ((), ())), preferred_element_type=f32
                )
                for b in range(2):
                    csum[2 * h + b, u, pl.ds(q, 1), :] = jnp.sum(
                        mixed[:, b * unit:(b + 1) * unit] * g_all[2 * h + b, u].astype(f32), axis=0, keepdims=True
                    )
            return carry

        lax.fori_loop(0, len(which), body, 0)

    def loaded(*which):
        for n in which:
            loads[n].wait()

    meet()
    og[0].begin()
    scale_all()
    og[0].relay()
    og[1].begin()
    og[0].near()
    og[2].begin()
    loaded(0, 4)
    og[0].paired()
    project_near(0)
    og[0].far()
    og[0].finish()
    project(0)
    og[1].relay()
    act[0].begin()
    og[1].near()
    og[1].paired()
    project_near(1)
    service(1, 0)
    og[1].far()
    og[2].relay()
    act[1].begin()
    og[2].near()
    og[1].finish()
    project(1)
    service(2, 0)
    act[0].relay()
    act[2].begin()
    act[0].near()
    og[2].paired()
    project_near(2)
    og[2].far()
    og[2].finish()
    service(1, 1)
    project(2)
    service(3, 0)
    loaded(1, 5)
    service(2, 1)
    act[0].far()
    act[0].paired()
    act[0].finish()
    act[1].relay()
    act[1].near()
    contract(0)
    spread(0)
    service(1, 2)
    act[2].relay()
    act[2].near()
    og[3].open()
    act[1].far()
    act[1].paired()
    act[1].finish()
    contract(1)
    spread(1)
    lift(0)
    act[2].far()
    act[2].paired()
    act[2].finish()
    contract(2)
    spread(2)
    og[3].extend()
    service(2, 2)
    service(3, 1)
    lift(1)
    lifted(0)
    og[0].drain()
    acts[0].begin()
    og[3].relay()
    lift(2)
    og[3].near()
    og[3].paired()
    project_near(3)
    acts[0].relay()
    og[1].drain()
    acts[1].begin()
    acts[0].near()
    og[3].far()
    lifted(1)
    og[2].drain()
    acts[2].begin()
    og[3].finish()
    acts[0].far()
    project(3)
    acts[0].paired()
    acts[0].finish()
    acts[1].relay()
    score(0, 0)
    act[0].drain()
    acts[3].begin()
    acts[1].near()
    score(1, 0)
    acts[2].relay()
    acts[2].near()
    lifted(2)
    act[1].drain()
    acts[4].begin()
    acts[1].far()
    service(1, 3)
    acts[1].paired()
    acts[1].finish()
    score(0, 1)
    acts[3].relay()
    acts[3].near()
    act[2].drain()
    acts[5].begin()
    acts[2].far()
    service(1, 4)
    score(1, 1)
    acts[2].paired()
    acts[2].finish()
    score(0, 2)
    acts[4].relay()
    acts[4].near()
    acts[3].far()
    service(3, 2)
    score(1, 2)
    service(2, 3)
    acts[3].paired()
    acts[3].finish()
    score(0, 3)
    acts[5].relay()
    acts[5].near()
    acts[4].far()
    service(2, 4)
    score(1, 3)
    acts[4].paired()
    acts[4].finish()
    score(0, 4)
    acts[5].far()
    service(3, 3)
    score(1, 4)
    acts[5].paired()
    acts[5].finish()
    score(0, 5)
    service(3, 4)
    score(1, 5)
    per = res_ref.shape[1]
    lane_at = lax.broadcasted_iota(jnp.int32, (8, per), 1)
    for b in range(planes):
        tile = jnp.zeros((8, per), f32)
        for u in range(units):
            total = jnp.sum(csum[b, u], axis=1, keepdims=True)
            tile = tile + jnp.where(lane_at == u, total, 0.0)
        tiles[b] = tile

    def fold(to):
        return pltpu.make_async_remote_copy(
            src_ref=tiles.at[to], dst_ref=got_z.at[z], send_sem=rz_send.at[0], recv_sem=rz_recv.at[0],
            device_id={"dp": to}, device_id_type=MESH,
        )

    def folds():
        view = got_z.at[pl.ds(0, planes - 1)]
        return pltpu.make_async_remote_copy(
            src_ref=view, dst_ref=view, send_sem=rz_send.at[0], recv_sem=rz_recv.at[0],
            device_id={"dp": lax.rem(z + 1, planes)}, device_id_type=MESH,
        )

    def fold_all():
        for step in range(1, planes):
            fold(lax.rem(z + step, planes)).start()
        got_z[z] = tiles[z]
        folds().wait_recv()
        total = got_z[0]
        for b in range(1, planes):
            total = total + got_z[b]
        got_p[j] = total

    def share(to):
        return pltpu.make_async_remote_copy(
            src_ref=got_p.at[j], dst_ref=got_p.at[j], send_sem=rp_send.at[0], recv_sem=rp_recv.at[0],
            device_id={"tensor": to}, device_id_type=MESH,
        )

    def shares():
        view = got_p.at[pl.ds(0, members - 1)]
        return pltpu.make_async_remote_copy(
            src_ref=view, dst_ref=view, send_sem=rp_send.at[0], recv_sem=rp_recv.at[0],
            device_id={"tensor": jp}, device_id_type=MESH,
        )

    def share_all():
        for step in range(1, members):
            share(lax.rem(j + step, members)).start()
        shares().wait_recv()
        total = got_p[0]
        for k in range(1, members):
            total = total + got_p[k]
        res_ref[...] = total

    def drain_all():
        for op in og[pairs:] + acts:
            op.drain()
        for level in range(planes):
            @pl.when((z - level >= 0) & (z < planes - 1))
            def _():
                whole(z - level, up_send, ch_recv).wait_send()

            @pl.when((z + level < planes) & (z > 0))
            def _():
                whole(z + level, dn_send, ch_recv).wait_send()
        for r in range(pairs):
            spreads(r, members - 1).wait_send()
            lifts(r).wait_send()
        folds().wait_send()
        shares().wait_send()

    fold_all()
    share_all()
    drain_all()


def fits(planes, members, activations, out_grads_t, in_basis, query_proj, seq_count):
    rows, feats = activations.shape
    width, tokens = out_grads_t.shape
    cols, span = in_basis.shape[1], query_proj.shape[2]
    unit = rows // seq_count
    return (
        members == 8 and planes == 4 and rows == tokens and rows == unit * seq_count and unit == 16 * members
        and seq_count == 6 and feats % 128 == 0 and cols % 128 == 0 and span % cols == 0 and span == 2 * cols
        and (members * width) // (6 * unit) == members // 2 * width // (6 * unit) - (-(members // 2) * width // (6 * unit))
        and width % 16 == 0 and width > 32 and query_proj.shape[0] <= 8
    )


def local(planes, members, activations, out_grads_t, in_basis, out_basis_t, query_proj, eigvals, damping, lengths):
    seq_count = lengths.shape[0]
    if not fits(planes, members, activations, out_grads_t, in_basis, query_proj, seq_count):
        return generic(activations, out_grads_t, in_basis, out_basis_t, query_proj, eigvals, damping, lengths)
    bf16, f32 = jnp.bfloat16, jnp.float32
    rows, feats = activations.shape
    width, tokens = out_grads_t.shape
    features, cols = in_basis.shape
    depth = out_basis_t.shape[1]
    queries, _, span = query_proj.shape
    unit = rows // seq_count
    part, pairs, group = unit // members, seq_count // 2, span // cols
    pieces = pairs + 1
    ops = pieces + pairs
    any_space = pl.BlockSpec(memory_space=pl.ANY)
    vmem = pl.BlockSpec(memory_space=pltpu.VMEM)
    smem = pl.BlockSpec(memory_space=pltpu.SMEM)
    dma = pltpu.SemaphoreType.DMA
    res = pl.pallas_call(
        kernel,
        out_shape=jax.ShapeDtypeStruct((8, 128), f32),
        in_specs=[any_space] * 6 + [smem, smem],
        out_specs=vmem,
        scratch_shapes=[
            pltpu.VMEM((members * width, tokens), bf16),
            pltpu.VMEM((members, rows, feats), bf16),
            pltpu.VMEM((features, cols), bf16),
            pltpu.VMEM((width, depth), bf16),
            pltpu.VMEM((queries, width, span), bf16),
            pltpu.VMEM((width, span), f32),
            pltpu.VMEM((seq_count, planes, unit, span), bf16),
            pltpu.VMEM((pairs, members, 2, part, cols), bf16),
            pltpu.VMEM((seq_count, unit, cols), bf16),
            pltpu.VMEM((2 * unit, cols), f32),
            pltpu.VMEM((planes, seq_count, width, unit), bf16),
            pltpu.VMEM((width, 2 * unit), f32),
            pltpu.VMEM((planes, seq_count, 8, unit), f32),
            pltpu.VMEM((planes, 8, 128), f32),
            pltpu.VMEM((planes, 8, 128), f32),
            pltpu.VMEM((members, 8, 128), f32),
            dma((6,)), dma((ops,)), dma((ops, 6)),
            dma((planes,)), dma((planes,)), dma((planes, pieces + 1)),
            dma((pairs,)), dma((pairs,)), dma((pairs,)), dma((pairs,)),
            dma((1,)), dma((1,)), dma((1,)), dma((1,)),
        ],
        compiler_params=pltpu.CompilerParams(
            collective_id=0, has_side_effects=True, vmem_limit_bytes=63 * 1024 * 1024
        ),
    )(activations, out_grads_t, in_basis, out_basis_t, query_proj, eigvals, lengths, damping)
    norm_factor = (features * depth * unit) ** (-0.5)
    return res[:queries, :seq_count].T * norm_factor


def solution(mesh):
    placed = (
        P("dp", "tensor"),
        P("tensor", "dp"),
        P(None, "tensor"),
        P("tensor", None),
        P(None, "tensor", "dp"),
        P("tensor", "dp"),
        P(),
        P("dp"),
    )
    return jax.shard_map(
        functools.partial(local, mesh.shape["dp"], mesh.shape["tensor"]), mesh=mesh, in_specs=placed, out_specs=P("dp", None), check_vma=False
    )
```
